32 devices in a mesh: seqs: 2 (over y), ctx: 4 (over z), head: 2 (over x), sub: 2 (over core).
Axes of the slice: x: 2, y: 2, z: 4, core: 2. Of those that a mesh axis runs over, the one named last changes fastest.
Arguments:
- streams: bfloat16 [3, 256, 4096], P(None, ('seqs', 'ctx'), ('head', 'sub')), parts along dimension 1, may hold values from -6 to 6
- history: bfloat16 [254, 4096], P('seqs', ('head', 'sub')), parts along dimension 0, may hold values from -6 to 6
- filters: bfloat16 [256, 128], P(('head', 'sub')), may hold values from -0.5 to 0.5
- skip_weight: bfloat16 [4096], P(('head', 'sub')), may hold values from -4 to 4
- offset: int32 [2], P('seqs'), parts along dimension 0, may hold values from 4096 to 36863
- lengths: int32 [8], P(('seqs', 'ctx')), parts along dimension 0, may hold values from 256 to 1024, as said below
- queries: bfloat16 [256, 4096], P(('seqs', 'ctx'), ('head', 'sub')), parts along dimension 0, may hold values from -160 to 160
- block_kv: bfloat16 [2, 256, 4096], P(None, ('seqs', 'ctx'), ('head', 'sub')), parts along dimension 1, may hold values from -7.5 to 7.5
- cache_keys: bfloat16 [8192, 4096], P(('seqs', 'ctx'), ('head', 'sub')), parts along dimension 0, may hold values from -20 to 20
- cache_values: bfloat16 [8192, 4096], P(('seqs', 'ctx'), ('head', 'sub')), parts along dimension 0, may hold values from -6 to 6
Outputs:
- hyena_out: bfloat16 [256, 4096], P(('seqs', 'ctx'), ('head', 'sub')), parts along dimension 0
- attended: bfloat16 [256, 4096], P(('seqs', 'ctx'), ('head', 'sub')), parts along dimension 0
The draws below stay inside these ranges and needn't reach their ends.
There are 2 independent parts, one for each index of `seqs`. The reference program is written for one: setup_inputs(seed, part) draws one part's arguments, and reference() takes and returns one part's arrays. A program takes and returns all parts, laid end to end along the dimension named above; an argument that names none is the same for every part. Nothing has to cross between parts.
Inputs may be any that keep to these rules, and one draw needn't show every extreme that they name: `lengths`: in every draw some shard's cache is full and some other holds 256 valid slots.
All inputs are finite; a program needn't handle non-finite values.
Results may differ from the reference program's by a relative error of at most 0.0081.
Values may be sent and summed in bfloat16 or wider, within the bound.
A program may use at most 192 MiB of HBM per device.

```python
import math
import jax
import jax.numpy as jnp
from jax import lax

D = 4096
HEADS = 32
HDIM = 128
TAPS = 128
GROUP = 16
CACHE_DEV = 1024
BLOCK = 128
CACHE = 4096
GROUPS = 256
N_CTX = 4


def draw_queries(key, part):
    values = 3.0 * jax.random.truncated_normal(key, -6.0, 6.0, (BLOCK, HEADS * HDIM), jnp.float32)
    return values.astype(jnp.bfloat16)


def draw_cache_keys(key, part):
    values = jax.random.truncated_normal(key, -6.0, 6.0, (CACHE, HEADS * HDIM), jnp.float32)
    return values.astype(jnp.bfloat16)


def draw_lengths(key, part):
    key_base, key_full, key_low = jax.random.split(key, 3)
    drawn = jax.random.randint(key_base, (N_CTX,), CACHE_DEV // 4, CACHE_DEV + 1, dtype=jnp.int32)
    full_at = jax.random.randint(key_full, (), 0, N_CTX, dtype=jnp.int32)
    low_at = (full_at + jax.random.randint(key_low, (), 1, N_CTX, dtype=jnp.int32)) % N_CTX
    index = jnp.arange(N_CTX, dtype=jnp.int32)
    drawn = jnp.where(index == full_at, CACHE_DEV, jnp.where(index == low_at, CACHE_DEV // 4, drawn))
    return drawn.astype(jnp.int32)


def shard_levels(stream_key, dims, cuts, least, top_value):
    level = 1.0
    for position, parts in cuts:
        heights = jax.random.uniform(jax.random.fold_in(jax.random.fold_in(stream_key, 6), position), (parts,), jnp.float32, least / len(cuts), top_value / len(cuts))
        level = level * jnp.repeat(jnp.exp(heights), dims[position] // parts).reshape((-1,) + (1,) * (len(dims) - 1 - position))
    return level


def centred(key, dims, scale, limit, shards=(), kind=jnp.bfloat16):
    loudness = shard_levels(key, dims, shards, -0.22, 0.18) if shards else 1.0
    entries = jax.random.normal(key, dims, jnp.float32) * scale * loudness
    return jnp.minimum(jnp.maximum(entries, -limit), limit).astype(kind)


def setup_inputs(seed: int = 0, part: int = 0) -> dict:
    seeds = jax.random.split(jax.random.key(seed), 11)
    part_splits = jax.random.split(jax.random.fold_in(seeds[10], part), 11)
    streams = centred(part_splits[0], (3, BLOCK, D), 1.0, 6.0, ((1, 4), (2, 4)))
    history = centred(part_splits[1], (TAPS - 1, D), 1.0, 6.0, ((1, 4),))
    filters = centred(seeds[2], (GROUPS, TAPS), TAPS ** -0.5, 0.5, ((0, 4),))
    skip_weight = centred(seeds[3], (D,), 1.0, 4.0, ((0, 4),))
    offset = jax.random.randint(part_splits[4], (1,), CACHE, CACHE + 32768).astype(jnp.int32)
    lengths = draw_lengths(jax.random.fold_in(jax.random.fold_in(seeds[10], part), 71), part)
    queries = draw_queries(jax.random.fold_in(jax.random.fold_in(seeds[10], part), 71), part)
    block_kv = centred(part_splits[7], (2, BLOCK, HEADS * HDIM), 1.25, 7.5, ((1, 4), (2, 4)))
    cache_keys = draw_cache_keys(jax.random.fold_in(jax.random.fold_in(seeds[10], part), 71), part)
    cache_values = centred(part_splits[9], (CACHE, HEADS * HDIM), 1.0, 6.0, ((0, 4), (1, 4)))
    return dict(streams=streams, history=history, filters=filters, skip_weight=skip_weight, offset=offset, lengths=lengths, queries=queries, block_kv=block_kv, cache_keys=cache_keys, cache_values=cache_values)


rope_base = 1000000.0
masked_score = -1e+30

def frequencies(head_dim):
    return 1.0 / rope_base ** (jnp.arange(head_dim // 2, dtype=jnp.float32) * (2.0 / head_dim))

def rotate(values, angles):
    half_dim = values.shape[-1] // 2
    former = values[..., :half_dim]
    latter = values[..., half_dim:]
    cosine = jnp.cos(angles)[:, None, :]
    sine_part = jnp.sin(angles)[:, None, :]
    return jnp.concatenate([former * cosine - latter * sine_part, latter * cosine + former * sine_part], axis=-1)

def reference(streams, history, filters, skip_weight, offset, lengths, queries, block_kv, cache_keys, cache_values):
    gate_in = streams[0].astype(jnp.float32)
    filter_in = (streams[1].astype(jnp.float32) * streams[2].astype(jnp.float32)).astype(jnp.bfloat16)
    sequence = jnp.concatenate([history, filter_in], axis=0).astype(jnp.float32)
    tap_table = jnp.repeat(filters.astype(jnp.float32), GROUP, axis=0)

    def add_tap(tap_index, running):
        window = lax.dynamic_slice_in_dim(sequence, TAPS - 1 - tap_index, BLOCK, 0)
        column = lax.dynamic_index_in_dim(tap_table, tap_index, 1, keepdims=False)
        return running + window * column[None, :]
    conv = lax.fori_loop(0, TAPS, add_tap, jnp.zeros((BLOCK, D), jnp.float32))
    hyena_out = (gate_in * (conv + skip_weight.astype(jnp.float32)[None, :] * filter_in.astype(jnp.float32))).astype(jnp.bfloat16)
    positions = (offset[0] + jnp.arange(BLOCK, dtype=jnp.int32)).astype(jnp.float32)
    angles = positions[:, None] * frequencies(HDIM)[None, :]
    rotated_q = rotate(queries.astype(jnp.float32).reshape(BLOCK, HEADS, HDIM), angles).astype(jnp.bfloat16)
    rotated_k = rotate(block_kv[0].astype(jnp.float32).reshape(BLOCK, HEADS, HDIM), angles).astype(jnp.bfloat16)
    block_values = block_kv[1].reshape(BLOCK, HEADS, HDIM)
    stored_keys = cache_keys.reshape(CACHE, HEADS, HDIM)
    stored_values = cache_values.reshape(CACHE, HEADS, HDIM)
    rows_all = jnp.arange(CACHE, dtype=jnp.int32)
    cache_valid = rows_all % CACHE_DEV < lengths[rows_all // CACHE_DEV]
    causal = jnp.arange(BLOCK, dtype=jnp.int32)[:, None] >= jnp.arange(BLOCK, dtype=jnp.int32)[None, :]
    scale = 1.0 / math.sqrt(HDIM)

    def one_head(pieces):
        head_q, head_k, head_v, cached_k, cached_v = pieces
        score_cache = jnp.dot(head_q, cached_k.T, preferred_element_type=jnp.float32) * scale
        score_cache = jnp.where(cache_valid[None, :], score_cache, masked_score)
        score_block = jnp.dot(head_q, head_k.T, preferred_element_type=jnp.float32) * scale
        score_block = jnp.where(causal, score_block, masked_score)
        top = jnp.maximum(lax.optimization_barrier(jnp.max(score_cache, axis=1)), lax.optimization_barrier(jnp.max(score_block, axis=1)))
        weight_cache = jnp.exp(score_cache - top[:, None])
        weight_block = jnp.exp(score_block - top[:, None])
        total = lax.optimization_barrier(jnp.sum(weight_cache, axis=1)) + lax.optimization_barrier(jnp.sum(weight_block, axis=1))
        summed = jnp.dot(weight_cache.astype(jnp.bfloat16), cached_v, preferred_element_type=jnp.float32)
        summed = summed + jnp.dot(weight_block.astype(jnp.bfloat16), head_v, preferred_element_type=jnp.float32)
        return (summed / total[:, None]).astype(jnp.bfloat16)
    results = lax.map(one_head, (jnp.moveaxis(rotated_q, 1, 0), jnp.moveaxis(rotated_k, 1, 0), jnp.moveaxis(block_values, 1, 0), jnp.moveaxis(stored_keys, 1, 0), jnp.moveaxis(stored_values, 1, 0)))
    attended = jnp.moveaxis(results, 0, 1).reshape(BLOCK, HEADS * HDIM)
    return (hyena_out, attended)
```

```python
import functools
import math

import jax
import jax.numpy as jnp
from jax import lax
from jax.experimental import pallas as pl
from jax.experimental.pallas import tpu as pltpu
from jax.sharding import PartitionSpec as P

HDIM = 128
ROPE_BASE = 1000000.0
MASKED = -1e30
MESH = pl.DeviceIdType.MESH
F32 = jnp.float32
BF16 = jnp.bfloat16
LANES = 128
VMEM_LIMIT = 32 * 2**20
EXPONENT = math.log2(math.e) / math.sqrt(HDIM)


def cos_sin(x):
    quarter = jnp.floor(x * (2.0 / math.pi) + 0.5)
    r = x - quarter * 1.5703125
    r = r - quarter * 4.837512969970703125e-4
    r = r - quarter * 7.54978995489188216e-8
    z = r * r
    sine = ((-1.9515295891e-4 * z + 8.3321608736e-3) * z - 1.6666654611e-1) * z * r + r
    cosine = (
        ((2.443315711809948e-5 * z - 1.388731625493765e-3) * z + 4.166664568298827e-2) * z * z
        - 0.5 * z
        + 1.0
    )
    turn = quarter.astype(jnp.int32) & 3
    odd = (turn & 1) == 1
    cos_x = jnp.where(odd, sine, cosine)
    sin_x = jnp.where(odd, cosine, sine)
    cos_x = jnp.where((turn == 1) | (turn == 2), -cos_x, cos_x)
    sin_x = jnp.where(turn >= 2, -sin_x, sin_x)
    return cos_x, sin_x


def kernel(
    n,
    offset_ref,
    lengths_ref,
    streams_hbm,
    history_hbm,
    filters_hbm,
    skip_hbm,
    queries_hbm,
    kv_hbm,
    keys_hbm,
    values_hbm,
    both_ref,
    streams,
    history,
    filters,
    skip,
    queries,
    kv,
    keys,
    values,
    history_wide,
    extended,
    toeplitz,
    all_q,
    out_send,
    out_recv,
    stat_send,
    stat_recv,
    in_sems,
    q_send,
    q_recv,
    f_send,
    f_recv,
    o_send,
    o_recv,
    s_send,
    s_recv,
):
    me = lax.axis_index("ctx")
    rows, channels = queries.shape
    heads = channels // HDIM
    groups, taps = filters.shape
    cache_rows = keys_hbm.shape[0]
    span = keys.shape[0]
    tile_groups = LANES // (channels // groups)

    barrier = pltpu.get_barrier_semaphore()
    for i in range(1, n):
        pl.semaphore_signal(
            barrier, inc=1, device_id={"ctx": lax.rem(me + i, n)}, device_id_type=MESH
        )

    loads = [
        pltpu.make_async_copy(source, target, in_sems.at[i])
        for i, (source, target) in enumerate(
            [
                (queries_hbm, queries),
                (streams_hbm, streams),
                (kv_hbm, kv),
                (filters_hbm, filters),
                (history_hbm, history),
                (skip_hbm, skip),
                (keys_hbm, keys.at[pl.ds(0, cache_rows)]),
                (values_hbm, values.at[pl.ds(0, cache_rows)]),
            ]
        )
    ]
    for load in loads:
        load.start()

    position = (
        offset_ref[0] + me * rows + lax.broadcasted_iota(jnp.int32, (rows, HDIM), 0)
    ).astype(F32)
    lane = lax.broadcasted_iota(jnp.int32, (rows, HDIM), 1)
    pair = lax.broadcasted_iota(jnp.int32, (8, HDIM), 1) % (HDIM // 2)
    freq = jnp.ones((8, HDIM), F32)
    for i in range(1, HDIM // 2):
        freq = jnp.where(pair == i, float(1.0 / ROPE_BASE ** (2.0 * i / HDIM)), freq)
    cosine, sine = cos_sin(position * freq[0:1, :])
    sine = jnp.where(lane < HDIM // 2, -sine, sine)

    def rotated(x):
        x = x.astype(F32)
        return (x * cosine + pltpu.roll(x, HDIM // 2, 1) * sine).astype(BF16)

    loads[0].wait()
    for h in range(heads):
        part = slice(h * HDIM, (h + 1) * HDIM)
        all_q[me, :, part] = rotated(queries[:, part])

    pl.semaphore_wait(barrier, n - 1)

    def flipped(i):
        result = me
        for b in [1 << k for k in range(n.bit_length()) if i >> k & 1]:
            result = result + b * (1 - 2 * lax.rem(lax.div(me, b), 2))
        return result

    def children(i):
        low = i & -i if i else n
        return [i + (1 << k) for k in reversed(range(n.bit_length())) if (1 << k) < low]

    def q_copy(i):
        low = i & -i
        block = flipped(i - low)
        return pltpu.make_async_remote_copy(
            src_ref=all_q.at[block],
            dst_ref=all_q.at[block],
            send_sem=q_send.at[i],
            recv_sem=q_recv.at[i],
            device_id={"ctx": flipped(low)},
            device_id_type=MESH,
        )

    for i in children(0):
        q_copy(i).start()

    loads[1].wait()
    own_rows = pl.ds(pl.multiple_of(taps + me * rows, rows), rows)
    extended[own_rows, :] = (streams[1].astype(F32) * streams[2].astype(F32)).astype(BF16)

    def f_copy(i):
        low = i & -i
        start = pl.multiple_of(taps + flipped(i - low) * rows, rows)
        return pltpu.make_async_remote_copy(
            src_ref=extended.at[pl.ds(start, rows)],
            dst_ref=extended.at[pl.ds(start, rows)],
            send_sem=f_send.at[i],
            recv_sem=f_recv.at[i],
            device_id={"ctx": flipped(low)},
            device_id_type=MESH,
        )

    def f_start(i):
        low = i & -i

        @pl.when(flipped(i - low) < flipped(low))
        def _():
            f_copy(i).start()

    def f_take(i):
        @pl.when(flipped(i) < me)
        def _():
            f_copy(i).wait_recv()

        for j in children(i):
            f_start(j)

    def q_take(i):
        q_copy(i).wait_recv()
        for j in children(i):
            q_copy(j).start()

    for i in children(0):
        f_start(i)

    loads[2].wait()
    for h in range(heads):
        part = slice(h * HDIM, (h + 1) * HDIM)
        keys[pl.ds(cache_rows, rows), part] = rotated(kv[0, :, part])
    values[pl.ds(cache_rows, rows), :] = kv[1]
    pad = span - cache_rows - rows
    keys[pl.ds(cache_rows + rows, pad), :] = jnp.zeros((pad, channels), BF16)
    values[pl.ds(cache_rows + rows, pad), :] = jnp.zeros((pad, channels), BF16)

    loads[3].wait()
    mirror = (
        lax.broadcasted_iota(jnp.int32, (taps, 2 * taps), 1)
        + lax.broadcasted_iota(jnp.int32, (taps, 2 * taps), 0)
        == taps
    ).astype(BF16)
    base = jnp.dot(filters[...], mirror, preferred_element_type=F32)
    for g in range(groups):
        line = jnp.broadcast_to(base[g : g + 1, :], (rows, 2 * taps))
        toeplitz[g * rows : (g + 1) * rows, :] = pltpu.roll(
            line, 0, 1, stride=1, stride_axis=0
        ).astype(BF16)

    loads[4].wait()
    history_wide[0:1, :] = jnp.zeros((1, channels), F32)
    history_wide[1:taps, :] = history[...].astype(F32)
    extended[0:taps, :] = history_wide[...].astype(BF16)
    loads[5].wait()

    loads[6].wait()
    loads[7].wait()
    column = lax.broadcasted_iota(jnp.int32, (rows, span), 1)
    token = lax.broadcasted_iota(jnp.int32, (rows, span), 0)
    length = lengths_ref[0]

    def attend(source):
        kept = (column < jnp.minimum(length, cache_rows)) | (
            (column >= cache_rows)
            & (column < cache_rows + rows)
            & (column - cache_rows + me * rows <= token + source * rows)
        )
        bias = jnp.where(kept, 0.0, MASKED)
        stat = jnp.zeros((rows, LANES), F32)
        parts = [slice(h * HDIM, (h + 1) * HDIM) for h in range(heads)]
        scores = [
            lax.dot_general(
                all_q[source, :, part],
                keys[:, part],
                (((1,), (1,)), ((), ())),
                preferred_element_type=F32,
            )
            + bias
            for part in parts
        ]
        tops = [jnp.max(score, axis=1, keepdims=True) for score in scores]
        weights = [
            jnp.exp2((score - top) * EXPONENT) for score, top in zip(scores, tops)
        ]
        totals = [jnp.sum(weight, axis=1, keepdims=True) for weight in weights]
        sums = [
            jnp.dot(weight.astype(BF16), values[:, part], preferred_element_type=F32)
            for weight, part in zip(weights, parts)
        ]
        for h in range(heads):
            out_send[source, :, parts[h]] = (sums[h] / totals[h]).astype(BF16)
            stat = jnp.where(lane == h, tops[h], stat)
            stat = jnp.where(lane == heads + h, totals[h], stat)
        packed = stat[0:8]
        for a in range(1, rows // 8):
            packed = packed + pltpu.roll(stat[8 * a : 8 * a + 8], 2 * heads * a, 1)
        stat_send[source] = packed

    def o_copy(i, source):
        return pltpu.make_async_remote_copy(
            src_ref=out_send.at[source],
            dst_ref=out_recv.at[me],
            send_sem=o_send.at[i],
            recv_sem=o_recv.at[i],
            device_id={"ctx": source},
            device_id_type=MESH,
        )

    def s_copy(i, source):
        return pltpu.make_async_remote_copy(
            src_ref=stat_send.at[source],
            dst_ref=stat_recv.at[me],
            send_sem=s_send.at[i],
            recv_sem=s_recv.at[i],
            device_id={"ctx": source},
            device_id_type=MESH,
        )

    def attend_and_send(i, source):
        attend(source)
        s_copy(i, source).start()
        o_copy(i, source).start()

    attend(me)
    if n == 4:
        q_take(2)
        q_take(1)
        attend_and_send(1, flipped(1))
        f_take(2)
        attend_and_send(2, flipped(2))
        q_take(3)
        attend_and_send(3, flipped(3))
        f_take(1)
        f_take(3)
    else:
        for i in sorted(range(1, n), key=lambda i: i.bit_count()):
            q_take(i)
            f_take(i)

        def step(i, _):
            attend_and_send(i, lax.rem(me - i + n, n))
            return 0

        lax.fori_loop(1, n, step, 0)

    direct = skip[...].astype(F32).reshape(1, channels)
    lane_group = lane // (channels // groups)
    for j in range(channels // LANES):
        part = slice(j * LANES, (j + 1) * LANES)
        stack = slice(j * tile_groups * rows, (j + 1) * tile_groups * rows)
        own = extended[own_rows, part]
        window = extended[pl.ds(pl.multiple_of(me * rows, rows), taps), part]
        product = jnp.dot(
            toeplitz[stack, 0:taps], window, preferred_element_type=F32
        ) + jnp.dot(toeplitz[stack, taps : taps + rows], own, preferred_element_type=F32)
        conv = product[0:rows]
        for g in range(1, tile_groups):
            conv = jnp.where(lane_group == g, product[g * rows : (g + 1) * rows], conv)
        both_ref[0, :, part] = (
            streams[0, :, part].astype(F32)
            * (conv + direct[:, part] * own.astype(F32))
        ).astype(BF16)

    for i in range(1, n):
        s_copy(i, me).wait_recv()

    stat_recv[me] = stat_send[me]
    def source_of(i):
        return flipped(i) if n == 4 else lax.rem(me + i, n)

    stats = []
    for i in range(n):
        packed = stat_recv[source_of(i)]
        stats.append(
            jnp.concatenate(
                [packed]
                + [
                    pltpu.roll(packed, LANES - 2 * heads * a, 1)
                    for a in range(1, rows // 8)
                ],
                axis=0,
            )
        )
    top = stats[0]
    for s in range(1, n):
        top = jnp.maximum(top, stats[s])
    shares = []
    whole = jnp.zeros((rows, LANES), F32)
    for s in range(n):
        stat = stats[s]
        count = pltpu.roll(stat, LANES - heads, 1)
        share = jnp.exp2((stat - top) * EXPONENT) * count
        share = jnp.where(lane < heads, share, 0.0)
        shares.append(share)
        whole = whole + share
    inverse = 1.0 / jnp.where(lane < heads, whole, 1.0)
    shares = [share * inverse for share in shares]
    merged = [jnp.zeros((rows, HDIM), F32)] * heads
    for i in range(n):
        if i:
            o_copy(i, me).wait_recv()
        came = out_recv.at[source_of(i)] if i else out_send.at[me]
        for h in range(heads):
            part = slice(h * HDIM, (h + 1) * HDIM)
            merged[h] = merged[h] + shares[i][:, h : h + 1] * came[:, part].astype(F32)
    for h in range(heads):
        both_ref[1, :, h * HDIM : (h + 1) * HDIM] = merged[h].astype(BF16)

    for i in range(1, n):
        q_copy(i).wait_send()
        o_copy(i, me).wait_send()
        s_copy(i, me).wait_send()
        low = i & -i

        @pl.when(flipped(i - low) < flipped(low))
        def _(i=i):
            f_copy(i).wait_send()


def shards(
    n,
    streams,
    history,
    filters,
    skip_weight,
    offset,
    lengths,
    queries,
    block_kv,
    cache_keys,
    cache_values,
):
    rows, channels = queries.shape
    groups, taps = filters.shape
    cache_rows = cache_keys.shape[0]
    span = cache_rows + LANES
    any_space = pl.BlockSpec(memory_space=pl.ANY)
    smem = pl.BlockSpec(memory_space=pltpu.SMEM)
    vmem = pl.BlockSpec(memory_space=pltpu.VMEM)
    dma = pltpu.SemaphoreType.DMA
    in_hbm = [
        pltpu.with_memory_space_constraint(x, pltpu.HBM)
        for x in (
            streams,
            history,
            filters,
            skip_weight,
            queries,
            block_kv,
            cache_keys,
            cache_values,
        )
    ]
    both = pl.pallas_call(
        functools.partial(kernel, n),
        out_shape=jax.ShapeDtypeStruct((2, rows, channels), BF16),
        in_specs=[smem, smem] + [any_space] * 8,
        out_specs=vmem,
        scratch_shapes=[
            pltpu.VMEM(streams.shape, BF16),
            pltpu.VMEM(history.shape, BF16),
            pltpu.VMEM(filters.shape, BF16),
            pltpu.VMEM((channels,), BF16),
            pltpu.VMEM((rows, channels), BF16),
            pltpu.VMEM(block_kv.shape, BF16),
            pltpu.VMEM((span, channels), BF16),
            pltpu.VMEM((span, channels), BF16),
            pltpu.VMEM((taps, channels), F32),
            pltpu.VMEM((taps + n * rows, channels), BF16),
            pltpu.VMEM((groups * rows, 2 * taps), BF16),
            pltpu.VMEM((n, rows, channels), BF16),
            pltpu.VMEM((n, rows, channels), BF16),
            pltpu.VMEM((n, rows, channels), BF16),
            pltpu.VMEM((n, 8, LANES), F32),
            pltpu.VMEM((n, 8, LANES), F32),
            dma((8,)),
            dma((n,)),
            dma((n,)),
            dma((n,)),
            dma((n,)),
            dma((n,)),
            dma((n,)),
            dma((n,)),
            dma((n,)),
        ],
        compiler_params=pltpu.CompilerParams(
            collective_id=0, has_side_effects=True, vmem_limit_bytes=VMEM_LIMIT
        ),
    )(
        offset,
        lengths,
        *in_hbm,
    )
    return both[0], both[1]


def solution(mesh):
    return jax.shard_map(
        functools.partial(shards, mesh.shape["ctx"]),
        mesh=mesh,
        in_specs=(
            P(None, ("seqs", "ctx"), ("head", "sub")),
            P("seqs", ("head", "sub")),
            P(("head", "sub"), None),
            P(("head", "sub")),
            P("seqs"),
            P(("seqs", "ctx")),
            P(("seqs", "ctx"), ("head", "sub")),
            P(None, ("seqs", "ctx"), ("head", "sub")),
            P(("seqs", "ctx"), ("head", "sub")),
            P(("seqs", "ctx"), ("head", "sub")),
        ),
        out_specs=(P(("seqs", "ctx"), ("head", "sub")), P(("seqs", "ctx"), ("head", "sub"))),
        check_vma=False,
    )
```

```python
import functools
import math

import jax
import jax.numpy as jnp
from jax import lax
from jax.experimental import pallas as pl
from jax.experimental.pallas import tpu as pltpu
from jax.sharding import PartitionSpec as P

HDIM = 128
ROPE_BASE = 1000000.0
MASKED = -1e30
MESH = pl.DeviceIdType.MESH
F32 = jnp.float32
BF16 = jnp.bfloat16
LANES = 128
CHUNKS = 2
VMEM_LIMIT = 32 * 2**20
EXPONENT = math.log2(math.e) / math.sqrt(HDIM)


def cos_sin(x):
    quarter = jnp.floor(x * (2.0 / math.pi) + 0.5)
    r = x - quarter * 1.5703125
    r = r - quarter * 4.837512969970703125e-4
    r = r - quarter * 7.54978995489188216e-8
    z = r * r
    sine = ((-1.9515295891e-4 * z + 8.3321608736e-3) * z - 1.6666654611e-1) * z * r + r
    cosine = (
        ((2.443315711809948e-5 * z - 1.388731625493765e-3) * z + 4.166664568298827e-2) * z * z
        - 0.5 * z
        + 1.0
    )
    turn = quarter.astype(jnp.int32) & 3
    odd = (turn & 1) == 1
    cos_x = jnp.where(odd, sine, cosine)
    sin_x = jnp.where(odd, cosine, sine)
    cos_x = jnp.where((turn == 1) | (turn == 2), -cos_x, cos_x)
    sin_x = jnp.where(turn >= 2, -sin_x, sin_x)
    return cos_x, sin_x


def kernel(
    n,
    offset_ref,
    lengths_ref,
    streams_hbm,
    history_hbm,
    filters_hbm,
    skip_hbm,
    queries_hbm,
    kv_hbm,
    keys_hbm,
    values_hbm,
    both_ref,
    streams,
    history,
    filters,
    skip,
    queries,
    kv,
    keys,
    values,
    history_wide,
    extended,
    toeplitz,
    all_q,
    out_send,
    out_recv,
    stat_send,
    stat_recv,
    in_sems,
    q_send,
    q_recv,
    f_send,
    f_recv,
    o_send,
    o_recv,
    s_send,
    s_recv,
):
    me = lax.axis_index("ctx")
    rows, channels = queries.shape
    heads = channels // HDIM
    groups, taps = filters.shape
    cache_rows = keys_hbm.shape[0]
    span = keys.shape[0]
    tile_groups = LANES // (channels // groups)

    barrier = pltpu.get_barrier_semaphore()
    for i in range(1, n):
        pl.semaphore_signal(
            barrier, inc=1, device_id={"ctx": lax.rem(me + i, n)}, device_id_type=MESH
        )

    loads = [
        pltpu.make_async_copy(source, target, in_sems.at[i])
        for i, (source, target) in enumerate(
            [
                (queries_hbm, queries),
                (streams_hbm, streams),
                (kv_hbm, kv),
                (filters_hbm, filters),
                (history_hbm, history),
                (skip_hbm, skip),
                (keys_hbm, keys.at[pl.ds(0, cache_rows)]),
                (values_hbm, values.at[pl.ds(0, cache_rows)]),
            ]
        )
    ]
    for load in loads:
        load.start()

    position = (
        offset_ref[0] + me * rows + lax.broadcasted_iota(jnp.int32, (rows, HDIM), 0)
    ).astype(F32)
    lane = lax.broadcasted_iota(jnp.int32, (rows, HDIM), 1)
    pair = lax.broadcasted_iota(jnp.int32, (8, HDIM), 1) % (HDIM // 2)
    freq = jnp.ones((8, HDIM), F32)
    for i in range(1, HDIM // 2):
        freq = jnp.where(pair == i, float(1.0 / ROPE_BASE ** (2.0 * i / HDIM)), freq)
    cosine, sine = cos_sin(position * freq[0:1, :])
    sine = jnp.where(lane < HDIM // 2, -sine, sine)

    def rotated(x):
        x = x.astype(F32)
        return (x * cosine + pltpu.roll(x, HDIM // 2, 1) * sine).astype(BF16)

    loads[0].wait()
    for h in range(heads):
        part = slice(h * HDIM, (h + 1) * HDIM)
        all_q[me, :, part] = rotated(queries[:, part])

    pl.semaphore_wait(barrier, n - 1)

    def flipped(i):
        result = me
        for b in [1 << k for k in range(n.bit_length()) if i >> k & 1]:
            result = result + b * (1 - 2 * lax.rem(lax.div(me, b), 2))
        return result

    def children(i):
        low = i & -i if i else n
        return [i + (1 << k) for k in reversed(range(n.bit_length())) if (1 << k) < low]

    def q_copy(i):
        low = i & -i
        block = flipped(i - low)
        return pltpu.make_async_remote_copy(
            src_ref=all_q.at[block],
            dst_ref=all_q.at[block],
            send_sem=q_send.at[i],
            recv_sem=q_recv.at[i],
            device_id={"ctx": flipped(low)},
            device_id_type=MESH,
        )

    for i in children(0):
        q_copy(i).start()

    loads[1].wait()
    own_rows = pl.ds(pl.multiple_of(taps + me * rows, rows), rows)
    extended[own_rows, :] = (streams[1].astype(F32) * streams[2].astype(F32)).astype(BF16)

    def f_copy(i):
        low = i & -i
        start = pl.multiple_of(taps + flipped(i - low) * rows, rows)
        return pltpu.make_async_remote_copy(
            src_ref=extended.at[pl.ds(start, rows)],
            dst_ref=extended.at[pl.ds(start, rows)],
            send_sem=f_send.at[i],
            recv_sem=f_recv.at[i],
            device_id={"ctx": flipped(low)},
            device_id_type=MESH,
        )

    def f_start(i):
        low = i & -i

        @pl.when(flipped(i - low) < flipped(low))
        def _():
            f_copy(i).start()

    def f_take(i):
        @pl.when(flipped(i) < me)
        def _():
            f_copy(i).wait_recv()

        for j in children(i):
            f_start(j)

    def q_take(i):
        q_copy(i).wait_recv()
        for j in children(i):
            q_copy(j).start()

    for i in children(0):
        f_start(i)

    loads[2].wait()
    for h in range(heads):
        part = slice(h * HDIM, (h + 1) * HDIM)
        keys[pl.ds(cache_rows, rows), part] = rotated(kv[0, :, part])
    values[pl.ds(cache_rows, rows), :] = kv[1]
    pad = span - cache_rows - rows
    keys[pl.ds(cache_rows + rows, pad), :] = jnp.zeros((pad, channels), BF16)
    values[pl.ds(cache_rows + rows, pad), :] = jnp.zeros((pad, channels), BF16)

    loads[3].wait()
    mirror = (
        lax.broadcasted_iota(jnp.int32, (taps, 2 * taps), 1)
        + lax.broadcasted_iota(jnp.int32, (taps, 2 * taps), 0)
        == taps
    ).astype(BF16)
    base = jnp.dot(filters[...], mirror, preferred_element_type=F32)
    for g in range(groups):
        line = jnp.broadcast_to(base[g : g + 1, :], (rows, 2 * taps))
        toeplitz[g * rows : (g + 1) * rows, :] = pltpu.roll(
            line, 0, 1, stride=1, stride_axis=0
        ).astype(BF16)

    loads[4].wait()
    history_wide[0:1, :] = jnp.zeros((1, channels), F32)
    history_wide[1:taps, :] = history[...].astype(F32)
    extended[0:taps, :] = history_wide[...].astype(BF16)
    loads[5].wait()

    loads[6].wait()
    loads[7].wait()
    column = lax.broadcasted_iota(jnp.int32, (rows, span), 1)
    token = lax.broadcasted_iota(jnp.int32, (rows, span), 0)
    length = lengths_ref[0]

    def attend(source):
        kept = (column < jnp.minimum(length, cache_rows)) | (
            (column >= cache_rows)
            & (column < cache_rows + rows)
            & (column - cache_rows + me * rows <= token + source * rows)
        )
        bias = jnp.where(kept, 0.0, MASKED)
        stat = jnp.zeros((rows, LANES), F32)
        parts = [slice(h * HDIM, (h + 1) * HDIM) for h in range(heads)]
        scores = [
            lax.dot_general(
                all_q[source, :, part],
                keys[:, part],
                (((1,), (1,)), ((), ())),
                preferred_element_type=F32,
            )
            + bias
            for part in parts
        ]
        tops = [jnp.max(score, axis=1, keepdims=True) for score in scores]
        weights = [
            jnp.exp2((score - top) * EXPONENT) for score, top in zip(scores, tops)
        ]
        totals = [jnp.sum(weight, axis=1, keepdims=True) for weight in weights]
        sums = [
            jnp.dot(weight.astype(BF16), values[:, part], preferred_element_type=F32)
            for weight, part in zip(weights, parts)
        ]
        for h in range(heads):
            out_send[source, :, parts[h]] = (sums[h] / totals[h]).astype(BF16)
            stat = jnp.where(lane == h, tops[h], stat)
            stat = jnp.where(lane == heads + h, totals[h], stat)
        packed = stat[0:8]
        for a in range(1, rows // 8):
            packed = packed + pltpu.roll(stat[8 * a : 8 * a + 8], 2 * heads * a, 1)
        stat_send[source] = packed

    def o_copy(i, source):
        return pltpu.make_async_remote_copy(
            src_ref=out_send.at[source],
            dst_ref=out_recv.at[me],
            send_sem=o_send.at[i],
            recv_sem=o_recv.at[i],
            device_id={"ctx": source},
            device_id_type=MESH,
        )

    def s_copy(i, source):
        return pltpu.make_async_remote_copy(
            src_ref=stat_send.at[source],
            dst_ref=stat_recv.at[me],
            send_sem=s_send.at[i],
            recv_sem=s_recv.at[i],
            device_id={"ctx": source},
            device_id_type=MESH,
        )

    def attend_and_send(i, source):
        attend(source)
        s_copy(i, source).start()
        o_copy(i, source).start()

    attend(me)
    if n == 4:
        q_take(2)
        q_take(1)
        attend_and_send(1, flipped(1))
        f_take(2)
        attend_and_send(2, flipped(2))
        q_take(3)
        attend_and_send(3, flipped(3))
        f_take(1)
        f_take(3)
    else:
        for i in sorted(range(1, n), key=lambda i: i.bit_count()):
            q_take(i)
            f_take(i)

        def step(i, _):
            attend_and_send(i, lax.rem(me - i + n, n))
            return 0

        lax.fori_loop(1, n, step, 0)

    direct = skip[...].astype(F32).reshape(1, channels)
    lane_group = lane // (channels // groups)
    for j in range(channels // LANES):
        part = slice(j * LANES, (j + 1) * LANES)
        stack = slice(j * tile_groups * rows, (j + 1) * tile_groups * rows)
        own = extended[own_rows, part]
        window = extended[pl.ds(pl.multiple_of(me * rows, rows), taps), part]
        product = jnp.dot(
            toeplitz[stack, 0:taps], window, preferred_element_type=F32
        ) + jnp.dot(toeplitz[stack, taps : taps + rows], own, preferred_element_type=F32)
        conv = product[0:rows]
        for g in range(1, tile_groups):
            conv = jnp.where(lane_group == g, product[g * rows : (g + 1) * rows], conv)
        both_ref[0, :, part] = (
            streams[0, :, part].astype(F32)
            * (conv + direct[:, part] * own.astype(F32))
        ).astype(BF16)

    for i in range(1, n):
        s_copy(i, me).wait_recv()

    stat_recv[me] = stat_send[me]
    def source_of(i):
        return flipped(i) if n == 4 else lax.rem(me + i, n)

    stats = []
    for i in range(n):
        packed = stat_recv[source_of(i)]
        stats.append(
            jnp.concatenate(
                [packed]
                + [
                    pltpu.roll(packed, LANES - 2 * heads * a, 1)
                    for a in range(1, rows // 8)
                ],
                axis=0,
            )
        )
    top = stats[0]
    for s in range(1, n):
        top = jnp.maximum(top, stats[s])
    shares = []
    whole = jnp.zeros((rows, LANES), F32)
    for s in range(n):
        stat = stats[s]
        count = pltpu.roll(stat, LANES - heads, 1)
        share = jnp.exp2((stat - top) * EXPONENT) * count
        share = jnp.where(lane < heads, share, 0.0)
        shares.append(share)
        whole = whole + share
    inverse = 1.0 / jnp.where(lane < heads, whole, 1.0)
    shares = [share * inverse for share in shares]
    merged = [jnp.zeros((rows, HDIM), F32)] * heads
    for i in range(n):
        if i:
            o_copy(i, me).wait_recv()
        came = out_recv.at[source_of(i)] if i else out_send.at[me]
        for h in range(heads):
            part = slice(h * HDIM, (h + 1) * HDIM)
            merged[h] = merged[h] + shares[i][:, h : h + 1] * came[:, part].astype(F32)
    for h in range(heads):
        both_ref[1, :, h * HDIM : (h + 1) * HDIM] = merged[h].astype(BF16)

    for i in range(1, n):
        q_copy(i).wait_send()
        o_copy(i, me).wait_send()
        s_copy(i, me).wait_send()
        low = i & -i

        @pl.when(flipped(i - low) < flipped(low))
        def _(i=i):
            f_copy(i).wait_send()


def kernel_of_four(
    offset_ref,
    lengths_ref,
    streams_hbm,
    history_hbm,
    filters_hbm,
    skip_hbm,
    queries_hbm,
    kv_hbm,
    keys_hbm,
    values_hbm,
    both_ref,
    streams,
    history,
    filters,
    skip,
    queries,
    kv,
    keys,
    values,
    keys_across,
    history_wide,
    extended,
    toeplitz,
    all_q,
    out_send,
    out_recv,
    stat_send,
    stat_recv,
    carry_send,
    carry,
    in_sems,
    q_send,
    q_recv,
    f_send,
    f_recv,
    o_send,
    o_recv,
    s_send,
    s_recv,
):
    n = 4
    me = lax.axis_index("ctx")
    rows, channels = queries.shape
    heads = channels // HDIM
    groups, taps = filters.shape
    cache_rows = keys_hbm.shape[0]
    span = keys.shape[0]
    tile_groups = LANES // (channels // groups)
    chunk = heads // CHUNKS

    near = me + 1 - 2 * lax.rem(me, 2)
    across = me + 2 - 4 * lax.div(me, 2)
    far = near + 2 - 4 * lax.div(near, 2)
    others = [near, across, far]

    barrier = pltpu.get_barrier_semaphore()
    for other in others:
        pl.semaphore_signal(
            barrier, inc=1, device_id={"ctx": other}, device_id_type=MESH
        )

    loads = [
        pltpu.make_async_copy(source, target, in_sems.at[i])
        for i, (source, target) in enumerate(
            [
                (queries_hbm, queries),
                (streams_hbm, streams),
                (kv_hbm, kv),
                (filters_hbm, filters),
                (history_hbm, history),
                (skip_hbm, skip),
                (keys_hbm, keys.at[pl.ds(0, cache_rows)]),
                (values_hbm, values.at[pl.ds(0, cache_rows)]),
            ]
        )
    ]
    for load in loads:
        load.start()

    position = (
        offset_ref[0] + me * rows + lax.broadcasted_iota(jnp.int32, (rows, HDIM), 0)
    ).astype(F32)
    lane = lax.broadcasted_iota(jnp.int32, (rows, HDIM), 1)
    pair = lax.broadcasted_iota(jnp.int32, (8, HDIM), 1) % (HDIM // 2)
    freq = jnp.ones((8, HDIM), F32)
    for i in range(1, HDIM // 2):
        freq = jnp.where(pair == i, float(1.0 / ROPE_BASE ** (2.0 * i / HDIM)), freq)
    cosine, sine = cos_sin(position * freq[0:1, :])
    sine = jnp.where(lane < HDIM // 2, -sine, sine)

    def rotated(x):
        x = x.astype(F32)
        return (x * cosine + pltpu.roll(x, HDIM // 2, 1) * sine).astype(BF16)

    def head(h):
        return slice(h * HDIM, (h + 1) * HDIM)

    loads[0].wait()
    for h in range(heads):
        all_q[me, h // chunk, :, head(h % chunk)] = rotated(queries[:, head(h)])

    pl.semaphore_wait(barrier, n - 1)

    def q_copy(kind, c):
        block = across if kind == 2 else me
        return pltpu.make_async_remote_copy(
            src_ref=all_q.at[block, c],
            dst_ref=all_q.at[block, c],
            send_sem=q_send.at[kind, c],
            recv_sem=q_recv.at[kind, c],
            device_id={"ctx": across if kind == 1 else near},
            device_id_type=MESH,
        )

    for c in range(CHUNKS):
        q_copy(1, c).start()
    for c in range(CHUNKS):
        q_copy(0, c).start()

    loads[1].wait()
    own_rows = pl.ds(pl.multiple_of(taps + me * rows, rows), rows)
    extended[own_rows, :] = (streams[1].astype(F32) * streams[2].astype(F32)).astype(BF16)

    passed = [(0, 1), (0, 2), (1, 2)]

    def f_copy(i):
        source, target = passed[i]
        block = extended.at[pl.ds(taps + source * rows, rows)]
        return pltpu.make_async_remote_copy(
            src_ref=block,
            dst_ref=block,
            send_sem=f_send.at[i],
            recv_sem=f_recv.at[i],
            device_id={"ctx": target},
            device_id_type=MESH,
        )

    def carry_copy():
        return pltpu.make_async_remote_copy(
            src_ref=carry_send,
            dst_ref=carry,
            send_sem=f_send.at[3],
            recv_sem=f_recv.at[3],
            device_id={"ctx": 3},
            device_id_type=MESH,
        )

    def on(device, action):
        pl.when(me == device)(action)

    def f_starts():
        on(0, lambda: (f_copy(1).start(), f_copy(0).start(), None)[-1])
        on(1, lambda: f_copy(2).start())

    f_starts()

    @pl.when(me == 3)
    def _():
        extended[taps : taps + 3 * rows, :] = jnp.zeros((3 * rows, channels), BF16)

    @pl.when(me != 3)
    def _():
        carry[...] = jnp.zeros((rows, channels), BF16)

    loads[2].wait()
    for h in range(heads):
        keys[pl.ds(cache_rows, rows), head(h)] = rotated(kv[0, :, head(h)])
    values[pl.ds(cache_rows, rows), :] = kv[1]
    pad = span - cache_rows - rows
    keys[pl.ds(cache_rows + rows, pad), :] = jnp.zeros((pad, channels), BF16)
    values[pl.ds(cache_rows + rows, pad), :] = jnp.zeros((pad, channels), BF16)

    loads[3].wait()
    mirror = (
        lax.broadcasted_iota(jnp.int32, (taps, 2 * taps), 1)
        + lax.broadcasted_iota(jnp.int32, (taps, 2 * taps), 0)
        == taps
    ).astype(BF16)
    base = jnp.dot(filters[...], mirror, preferred_element_type=F32)
    for g in range(groups):
        line = jnp.broadcast_to(base[g : g + 1, :], (rows, 2 * taps))
        toeplitz[g * rows : (g + 1) * rows, :] = pltpu.roll(
            line, 0, 1, stride=1, stride_axis=0
        ).astype(BF16)

    loads[4].wait()
    history_wide[0:1, :] = jnp.zeros((1, channels), F32)
    history_wide[1:taps, :] = history[...].astype(F32)
    extended[0:taps, :] = history_wide[...].astype(BF16)
    loads[5].wait()

    loads[6].wait()
    for h in range(heads):
        keys_across[head(h), :] = keys[:, head(h)].T
    loads[7].wait()
    length = lengths_ref[0]
    cached = lax.broadcasted_iota(jnp.int32, (8, cache_rows), 1)
    cache_bias = jnp.where(cached < length, 0.0, MASKED)[0:1, :]
    block_column = lax.broadcasted_iota(jnp.int32, (rows, span - cache_rows), 1)
    block_token = lax.broadcasted_iota(jnp.int32, (rows, span - cache_rows), 0)

    def attend(source, c, stat):
        kept = (block_column < rows) & (
            block_column + me * rows <= block_token + source * rows
        )
        block_bias = jnp.where(kept, 0.0, MASKED)
        mine = range(c * chunk, (c + 1) * chunk)
        scores = [
            jnp.dot(
                all_q[source, c, :, head(h - c * chunk)],
                keys_across[head(h), :],
                preferred_element_type=F32,
            )
            for h in mine
        ]
        scores = [
            jnp.concatenate(
                [score[:, :cache_rows] + cache_bias, score[:, cache_rows:] + block_bias],
                axis=1,
            )
            for score in scores
        ]
        tops = [jnp.max(score, axis=1, keepdims=True) for score in scores]
        weights = [
            jnp.exp2((score - top) * EXPONENT) for score, top in zip(scores, tops)
        ]
        totals = [jnp.sum(weight, axis=1, keepdims=True) for weight in weights]
        sums = [
            jnp.dot(weight.astype(BF16), values[:, head(h)], preferred_element_type=F32)
            for weight, h in zip(weights, mine)
        ]
        for i, h in enumerate(mine):
            out_send[source, c, :, head(i)] = (sums[i] / totals[i]).astype(BF16)
            stat = jnp.where(lane == h, tops[i], stat)
            stat = jnp.where(lane == heads + h, totals[i], stat)
        return stat

    def packed(stat):
        result = stat[0:8]
        for a in range(1, rows // 8):
            result = result + pltpu.roll(stat[8 * a : 8 * a + 8], 2 * heads * a, 1)
        return result

    def o_copy(kind, c):
        return pltpu.make_async_remote_copy(
            src_ref=out_send.at[others[kind], c],
            dst_ref=out_recv.at[me, c],
            send_sem=o_send.at[kind, c],
            recv_sem=o_recv.at[kind, c],
            device_id={"ctx": others[kind]},
            device_id_type=MESH,
        )

    def s_copy(kind):
        return pltpu.make_async_remote_copy(
            src_ref=stat_send.at[others[kind]],
            dst_ref=stat_recv.at[me],
            send_sem=s_send.at[kind],
            recv_sem=s_recv.at[kind],
            device_id={"ctx": others[kind]},
            device_id_type=MESH,
        )

    stats = [jnp.zeros((rows, LANES), F32)] * 3

    def attend_and_send(kind, c):
        stats[kind] = attend(others[kind], c, stats[kind])
        if c == CHUNKS - 1:
            stat_send[others[kind]] = packed(stats[kind])
            s_copy(kind).start()
        o_copy(kind, c).start()

    def conv_tile(j, window):
        stack = slice(j * tile_groups * rows, (j + 1) * tile_groups * rows)
        return jnp.dot(toeplitz[stack, 0:taps], window, preferred_element_type=F32)

    lane_group = lane // (channels // groups)

    def picked(product):
        conv = product[0:rows]
        for g in range(1, tile_groups):
            conv = jnp.where(lane_group == g, product[g * rows : (g + 1) * rows], conv)
        return conv

    def take_filter_inputs():
        on(1, lambda: f_copy(0).wait_recv())

        @pl.when(me == 2)
        def _():
            f_copy(1).wait_recv()
            f_copy(2).wait_recv()
            for j in range(channels // LANES):
                part = slice(j * LANES, (j + 1) * LANES)
                window = jnp.concatenate(
                    [
                        jnp.zeros((taps - 3 * rows, LANES), BF16),
                        extended[taps : taps + 3 * rows, part],
                    ],
                    axis=0,
                )
                carry_send[:, part] = picked(conv_tile(j, window)).astype(BF16)
            carry_copy().start()

    own = jnp.zeros((rows, LANES), F32)
    for c in range(CHUNKS):
        own = attend(me, c, own)
    stat_send[me] = packed(own)

    for c in range(CHUNKS):
        q_copy(1, c).wait_recv()
        q_copy(2, c).start()
        attend_and_send(1, c)
    for c in range(CHUNKS):
        q_copy(0, c).wait_recv()
        attend_and_send(0, c)
    take_filter_inputs()
    for c in range(CHUNKS):
        q_copy(2, c).wait_recv()
        attend_and_send(2, c)

    on(3, lambda: carry_copy().wait_recv())
    direct = skip[...].astype(F32).reshape(1, channels)
    for j in range(channels // LANES):
        part = slice(j * LANES, (j + 1) * LANES)
        stack = slice(j * tile_groups * rows, (j + 1) * tile_groups * rows)
        mine = extended[own_rows, part]
        window = extended[pl.ds(pl.multiple_of(me * rows, rows), taps), part]
        product = conv_tile(j, window) + jnp.dot(
            toeplitz[stack, taps : taps + rows], mine, preferred_element_type=F32
        )
        conv = picked(product) + carry[:, part].astype(F32)
        both_ref[0, :, part] = (
            streams[0, :, part].astype(F32)
            * (conv + direct[:, part] * mine.astype(F32))
        ).astype(BF16)

    for kind in range(3):
        s_copy(kind).wait_recv()

    def unpacked(value):
        return jnp.concatenate(
            [value]
            + [
                pltpu.roll(value, LANES - 2 * heads * a, 1) for a in range(1, rows // 8)
            ],
            axis=0,
        )

    came = [unpacked(stat_send[me])] + [unpacked(stat_recv[other]) for other in others]
    top = came[0]
    for stat in came[1:]:
        top = jnp.maximum(top, stat)
    shares = []
    whole = jnp.zeros((rows, LANES), F32)
    for stat in came:
        count = pltpu.roll(stat, LANES - heads, 1)
        share = jnp.exp2((stat - top) * EXPONENT) * count
        share = jnp.where(lane < heads, share, 0.0)
        shares.append(share)
        whole = whole + share
    inverse = 1.0 / jnp.where(lane < heads, whole, 1.0)
    shares = [share * inverse for share in shares]
    merged = [
        shares[0][:, h : h + 1]
        * out_send[me, h // chunk, :, head(h % chunk)].astype(F32)
        for h in range(heads)
    ]
    for kind in (0, 1, 2):
        for c in range(CHUNKS):
            o_copy(kind, c).wait_recv()
            for h in range(c * chunk, (c + 1) * chunk):
                merged[h] = merged[h] + shares[kind + 1][:, h : h + 1] * out_recv[
                    others[kind], c, :, head(h - c * chunk)
                ].astype(F32)
    for h in range(heads):
        both_ref[1, :, head(h)] = merged[h].astype(BF16)

    for kind in range(3):
        for c in range(CHUNKS):
            q_copy(kind, c).wait_send()
            o_copy(kind, c).wait_send()
        s_copy(kind).wait_send()
    on(0, lambda: (f_copy(0).wait_send(), f_copy(1).wait_send(), None)[-1])
    on(1, lambda: f_copy(2).wait_send())
    on(2, lambda: carry_copy().wait_send())


def four_shards(
    streams,
    history,
    filters,
    skip_weight,
    offset,
    lengths,
    queries,
    block_kv,
    cache_keys,
    cache_values,
):
    n = 4
    rows, channels = queries.shape
    groups, taps = filters.shape
    cache_rows = cache_keys.shape[0]
    span = cache_rows + LANES
    wide = channels // CHUNKS
    any_space = pl.BlockSpec(memory_space=pl.ANY)
    smem = pl.BlockSpec(memory_space=pltpu.SMEM)
    vmem = pl.BlockSpec(memory_space=pltpu.VMEM)
    dma = pltpu.SemaphoreType.DMA
    in_hbm = [
        pltpu.with_memory_space_constraint(x, pltpu.HBM)
        for x in (
            streams,
            history,
            filters,
            skip_weight,
            queries,
            block_kv,
            cache_keys,
            cache_values,
        )
    ]
    both = pl.pallas_call(
        kernel_of_four,
        out_shape=jax.ShapeDtypeStruct((2, rows, channels), BF16),
        in_specs=[smem, smem] + [any_space] * 8,
        out_specs=vmem,
        scratch_shapes=[
            pltpu.VMEM(streams.shape, BF16),
            pltpu.VMEM(history.shape, BF16),
            pltpu.VMEM(filters.shape, BF16),
            pltpu.VMEM((channels,), BF16),
            pltpu.VMEM((rows, channels), BF16),
            pltpu.VMEM(block_kv.shape, BF16),
            pltpu.VMEM((span, channels), BF16),
            pltpu.VMEM((span, channels), BF16),
            pltpu.VMEM((channels, span), BF16),
            pltpu.VMEM((taps, channels), F32),
            pltpu.VMEM((taps + n * rows, channels), BF16),
            pltpu.VMEM((groups * rows, 2 * taps), BF16),
            pltpu.VMEM((n, CHUNKS, rows, wide), BF16),
            pltpu.VMEM((n, CHUNKS, rows, wide), BF16),
            pltpu.VMEM((n, CHUNKS, rows, wide), BF16),
            pltpu.VMEM((n, 8, LANES), F32),
            pltpu.VMEM((n, 8, LANES), F32),
            pltpu.VMEM((rows, channels), BF16),
            pltpu.VMEM((rows, channels), BF16),
            dma((8,)),
            dma((3, CHUNKS)),
            dma((3, CHUNKS)),
            dma((4,)),
            dma((4,)),
            dma((3, CHUNKS)),
            dma((3, CHUNKS)),
            dma((3,)),
            dma((3,)),
        ],
        compiler_params=pltpu.CompilerParams(
            collective_id=0, has_side_effects=True, vmem_limit_bytes=VMEM_LIMIT
        ),
    )(
        offset,
        lengths,
        *in_hbm,
    )
    return both[0], both[1]


def shards(
    n,
    streams,
    history,
    filters,
    skip_weight,
    offset,
    lengths,
    queries,
    block_kv,
    cache_keys,
    cache_values,
):
    rows, channels = queries.shape
    groups, taps = filters.shape
    cache_rows = cache_keys.shape[0]
    span = cache_rows + LANES
    if n == 4:
        return four_shards(
            streams,
            history,
            filters,
            skip_weight,
            offset,
            lengths,
            queries,
            block_kv,
            cache_keys,
            cache_values,
        )
    any_space = pl.BlockSpec(memory_space=pl.ANY)
    smem = pl.BlockSpec(memory_space=pltpu.SMEM)
    vmem = pl.BlockSpec(memory_space=pltpu.VMEM)
    dma = pltpu.SemaphoreType.DMA
    in_hbm = [
        pltpu.with_memory_space_constraint(x, pltpu.HBM)
        for x in (
            streams,
            history,
            filters,
            skip_weight,
            queries,
            block_kv,
            cache_keys,
            cache_values,
        )
    ]
    both = pl.pallas_call(
        functools.partial(kernel, n),
        out_shape=jax.ShapeDtypeStruct((2, rows, channels), BF16),
        in_specs=[smem, smem] + [any_space] * 8,
        out_specs=vmem,
        scratch_shapes=[
            pltpu.VMEM(streams.shape, BF16),
            pltpu.VMEM(history.shape, BF16),
            pltpu.VMEM(filters.shape, BF16),
            pltpu.VMEM((channels,), BF16),
            pltpu.VMEM((rows, channels), BF16),
            pltpu.VMEM(block_kv.shape, BF16),
            pltpu.VMEM((span, channels), BF16),
            pltpu.VMEM((span, channels), BF16),
            pltpu.VMEM((taps, channels), F32),
            pltpu.VMEM((taps + n * rows, channels), BF16),
            pltpu.VMEM((groups * rows, 2 * taps), BF16),
            pltpu.VMEM((n, rows, channels), BF16),
            pltpu.VMEM((n, rows, channels), BF16),
            pltpu.VMEM((n, rows, channels), BF16),
            pltpu.VMEM((n, 8, LANES), F32),
            pltpu.VMEM((n, 8, LANES), F32),
            dma((8,)),
            dma((n,)),
            dma((n,)),
            dma((n,)),
            dma((n,)),
            dma((n,)),
            dma((n,)),
            dma((n,)),
            dma((n,)),
        ],
        compiler_params=pltpu.CompilerParams(
            collective_id=0, has_side_effects=True, vmem_limit_bytes=VMEM_LIMIT
        ),
    )(
        offset,
        lengths,
        *in_hbm,
    )
    return both[0], both[1]


def solution(mesh):
    return jax.shard_map(
        functools.partial(shards, mesh.shape["ctx"]),
        mesh=mesh,
        in_specs=(
            P(None, ("seqs", "ctx"), ("head", "sub")),
            P("seqs", ("head", "sub")),
            P(("head", "sub"), None),
            P(("head", "sub")),
            P("seqs"),
            P(("seqs", "ctx")),
            P(("seqs", "ctx"), ("head", "sub")),
            P(None, ("seqs", "ctx"), ("head", "sub")),
            P(("seqs", "ctx"), ("head", "sub")),
            P(("seqs", "ctx"), ("head", "sub")),
        ),
        out_specs=(P(("seqs", "ctx"), ("head", "sub")), P(("seqs", "ctx"), ("head", "sub"))),
        check_vma=False,
    )
```

```python
import functools
import math

import jax
import jax.numpy as jnp
from jax import lax
from jax.experimental import pallas as pl
from jax.experimental.pallas import tpu as pltpu
from jax.sharding import PartitionSpec as P

HDIM = 128
ROPE_BASE = 1000000.0
MASKED = -1e30
MESH = pl.DeviceIdType.MESH
F32 = jnp.float32
BF16 = jnp.bfloat16
LANES = 128
CHUNKS = 2
VMEM_LIMIT = 32 * 2**20
EXPONENT = math.log2(math.e) / math.sqrt(HDIM)


def cos_sin(x):
    quarter = jnp.floor(x * (2.0 / math.pi) + 0.5)
    r = x - quarter * 1.5703125
    r = r - quarter * 4.837512969970703125e-4
    r = r - quarter * 7.54978995489188216e-8
    z = r * r
    sine = ((-1.9515295891e-4 * z + 8.3321608736e-3) * z - 1.6666654611e-1) * z * r + r
    cosine = (
        ((2.443315711809948e-5 * z - 1.388731625493765e-3) * z + 4.166664568298827e-2) * z * z
        - 0.5 * z
        + 1.0
    )
    turn = quarter.astype(jnp.int32) & 3
    odd = (turn & 1) == 1
    cos_x = jnp.where(odd, sine, cosine)
    sin_x = jnp.where(odd, cosine, sine)
    cos_x = jnp.where((turn == 1) | (turn == 2), -cos_x, cos_x)
    sin_x = jnp.where(turn >= 2, -sin_x, sin_x)
    return cos_x, sin_x


def kernel(
    n,
    offset_ref,
    lengths_ref,
    streams_hbm,
    history_hbm,
    filters_hbm,
    skip_hbm,
    queries_hbm,
    kv_hbm,
    keys_hbm,
    values_hbm,
    both_ref,
    streams,
    history,
    filters,
    skip,
    queries,
    kv,
    keys,
    values,
    history_wide,
    extended,
    toeplitz,
    all_q,
    out_send,
    out_recv,
    stat_send,
    stat_recv,
    in_sems,
    q_send,
    q_recv,
    f_send,
    f_recv,
    o_send,
    o_recv,
    s_send,
    s_recv,
):
    me = lax.axis_index("ctx")
    rows, channels = queries.shape
    heads = channels // HDIM
    groups, taps = filters.shape
    cache_rows = keys_hbm.shape[0]
    span = keys.shape[0]
    tile_groups = LANES // (channels // groups)

    barrier = pltpu.get_barrier_semaphore()
    for i in range(1, n):
        pl.semaphore_signal(
            barrier, inc=1, device_id={"ctx": lax.rem(me + i, n)}, device_id_type=MESH
        )

    loads = [
        pltpu.make_async_copy(source, target, in_sems.at[i])
        for i, (source, target) in enumerate(
            [
                (queries_hbm, queries),
                (streams_hbm, streams),
                (kv_hbm, kv),
                (filters_hbm, filters),
                (history_hbm, history),
                (skip_hbm, skip),
                (keys_hbm, keys.at[pl.ds(0, cache_rows)]),
                (values_hbm, values.at[pl.ds(0, cache_rows)]),
            ]
        )
    ]
    for load in loads:
        load.start()

    position = (
        offset_ref[0] + me * rows + lax.broadcasted_iota(jnp.int32, (rows, HDIM), 0)
    ).astype(F32)
    lane = lax.broadcasted_iota(jnp.int32, (rows, HDIM), 1)
    pair = lax.broadcasted_iota(jnp.int32, (8, HDIM), 1) % (HDIM // 2)
    freq = jnp.ones((8, HDIM), F32)
    for i in range(1, HDIM // 2):
        freq = jnp.where(pair == i, float(1.0 / ROPE_BASE ** (2.0 * i / HDIM)), freq)
    cosine, sine = cos_sin(position * freq[0:1, :])
    sine = jnp.where(lane < HDIM // 2, -sine, sine)

    def rotated(x):
        x = x.astype(F32)
        return (x * cosine + pltpu.roll(x, HDIM // 2, 1) * sine).astype(BF16)

    loads[0].wait()
    for h in range(heads):
        part = slice(h * HDIM, (h + 1) * HDIM)
        all_q[me, :, part] = rotated(queries[:, part])

    pl.semaphore_wait(barrier, n - 1)

    def flipped(i):
        result = me
        for b in [1 << k for k in range(n.bit_length()) if i >> k & 1]:
            result = result + b * (1 - 2 * lax.rem(lax.div(me, b), 2))
        return result

    def children(i):
        low = i & -i if i else n
        return [i + (1 << k) for k in reversed(range(n.bit_length())) if (1 << k) < low]

    def q_copy(i):
        low = i & -i
        block = flipped(i - low)
        return pltpu.make_async_remote_copy(
            src_ref=all_q.at[block],
            dst_ref=all_q.at[block],
            send_sem=q_send.at[i],
            recv_sem=q_recv.at[i],
            device_id={"ctx": flipped(low)},
            device_id_type=MESH,
        )

    for i in children(0):
        q_copy(i).start()

    loads[1].wait()
    own_rows = pl.ds(pl.multiple_of(taps + me * rows, rows), rows)
    extended[own_rows, :] = (streams[1].astype(F32) * streams[2].astype(F32)).astype(BF16)

    def f_copy(i):
        low = i & -i
        start = pl.multiple_of(taps + flipped(i - low) * rows, rows)
        return pltpu.make_async_remote_copy(
            src_ref=extended.at[pl.ds(start, rows)],
            dst_ref=extended.at[pl.ds(start, rows)],
            send_sem=f_send.at[i],
            recv_sem=f_recv.at[i],
            device_id={"ctx": flipped(low)},
            device_id_type=MESH,
        )

    def f_start(i):
        low = i & -i

        @pl.when(flipped(i - low) < flipped(low))
        def _():
            f_copy(i).start()

    def f_take(i):
        @pl.when(flipped(i) < me)
        def _():
            f_copy(i).wait_recv()

        for j in children(i):
            f_start(j)

    def q_take(i):
        q_copy(i).wait_recv()
        for j in children(i):
            q_copy(j).start()

    for i in children(0):
        f_start(i)

    loads[2].wait()
    for h in range(heads):
        part = slice(h * HDIM, (h + 1) * HDIM)
        keys[pl.ds(cache_rows, rows), part] = rotated(kv[0, :, part])
    values[pl.ds(cache_rows, rows), :] = kv[1]
    pad = span - cache_rows - rows
    keys[pl.ds(cache_rows + rows, pad), :] = jnp.zeros((pad, channels), BF16)
    values[pl.ds(cache_rows + rows, pad), :] = jnp.zeros((pad, channels), BF16)

    loads[3].wait()
    mirror = (
        lax.broadcasted_iota(jnp.int32, (taps, 2 * taps), 1)
        + lax.broadcasted_iota(jnp.int32, (taps, 2 * taps), 0)
        == taps
    ).astype(BF16)
    base = jnp.dot(filters[...], mirror, preferred_element_type=F32)
    for g in range(groups):
        line = jnp.broadcast_to(base[g : g + 1, :], (rows, 2 * taps))
        toeplitz[g * rows : (g + 1) * rows, :] = pltpu.roll(
            line, 0, 1, stride=1, stride_axis=0
        ).astype(BF16)

    loads[4].wait()
    history_wide[0:1, :] = jnp.zeros((1, channels), F32)
    history_wide[1:taps, :] = history[...].astype(F32)
    extended[0:taps, :] = history_wide[...].astype(BF16)
    loads[5].wait()

    loads[6].wait()
    loads[7].wait()
    column = lax.broadcasted_iota(jnp.int32, (rows, span), 1)
    token = lax.broadcasted_iota(jnp.int32, (rows, span), 0)
    length = lengths_ref[0]

    def attend(source):
        kept = (column < jnp.minimum(length, cache_rows)) | (
            (column >= cache_rows)
            & (column < cache_rows + rows)
            & (column - cache_rows + me * rows <= token + source * rows)
        )
        bias = jnp.where(kept, 0.0, MASKED)
        stat = jnp.zeros((rows, LANES), F32)
        parts = [slice(h * HDIM, (h + 1) * HDIM) for h in range(heads)]
        scores = [
            lax.dot_general(
                all_q[source, :, part],
                keys[:, part],
                (((1,), (1,)), ((), ())),
                preferred_element_type=F32,
            )
            + bias
            for part in parts
        ]
        tops = [jnp.max(score, axis=1, keepdims=True) for score in scores]
        weights = [
            jnp.exp2((score - top) * EXPONENT) for score, top in zip(scores, tops)
        ]
        totals = [jnp.sum(weight, axis=1, keepdims=True) for weight in weights]
        sums = [
            jnp.dot(weight.astype(BF16), values[:, part], preferred_element_type=F32)
            for weight, part in zip(weights, parts)
        ]
        for h in range(heads):
            out_send[source, :, parts[h]] = (sums[h] / totals[h]).astype(BF16)
            stat = jnp.where(lane == h, tops[h], stat)
            stat = jnp.where(lane == heads + h, totals[h], stat)
        packed = stat[0:8]
        for a in range(1, rows // 8):
            packed = packed + pltpu.roll(stat[8 * a : 8 * a + 8], 2 * heads * a, 1)
        stat_send[source] = packed

    def o_copy(i, source):
        return pltpu.make_async_remote_copy(
            src_ref=out_send.at[source],
            dst_ref=out_recv.at[me],
            send_sem=o_send.at[i],
            recv_sem=o_recv.at[i],
            device_id={"ctx": source},
            device_id_type=MESH,
        )

    def s_copy(i, source):
        return pltpu.make_async_remote_copy(
            src_ref=stat_send.at[source],
            dst_ref=stat_recv.at[me],
            send_sem=s_send.at[i],
            recv_sem=s_recv.at[i],
            device_id={"ctx": source},
            device_id_type=MESH,
        )

    def attend_and_send(i, source):
        attend(source)
        s_copy(i, source).start()
        o_copy(i, source).start()

    attend(me)
    if n == 4:
        q_take(2)
        q_take(1)
        attend_and_send(1, flipped(1))
        f_take(2)
        attend_and_send(2, flipped(2))
        q_take(3)
        attend_and_send(3, flipped(3))
        f_take(1)
        f_take(3)
    else:
        for i in sorted(range(1, n), key=lambda i: i.bit_count()):
            q_take(i)
            f_take(i)

        def step(i, _):
            attend_and_send(i, lax.rem(me - i + n, n))
            return 0

        lax.fori_loop(1, n, step, 0)

    direct = skip[...].astype(F32).reshape(1, channels)
    lane_group = lane // (channels // groups)
    for j in range(channels // LANES):
        part = slice(j * LANES, (j + 1) * LANES)
        stack = slice(j * tile_groups * rows, (j + 1) * tile_groups * rows)
        own = extended[own_rows, part]
        window = extended[pl.ds(pl.multiple_of(me * rows, rows), taps), part]
        product = jnp.dot(
            toeplitz[stack, 0:taps], window, preferred_element_type=F32
        ) + jnp.dot(toeplitz[stack, taps : taps + rows], own, preferred_element_type=F32)
        conv = product[0:rows]
        for g in range(1, tile_groups):
            conv = jnp.where(lane_group == g, product[g * rows : (g + 1) * rows], conv)
        both_ref[0, :, part] = (
            streams[0, :, part].astype(F32)
            * (conv + direct[:, part] * own.astype(F32))
        ).astype(BF16)

    for i in range(1, n):
        s_copy(i, me).wait_recv()

    stat_recv[me] = stat_send[me]
    def source_of(i):
        return flipped(i) if n == 4 else lax.rem(me + i, n)

    stats = []
    for i in range(n):
        packed = stat_recv[source_of(i)]
        stats.append(
            jnp.concatenate(
                [packed]
                + [
                    pltpu.roll(packed, LANES - 2 * heads * a, 1)
                    for a in range(1, rows // 8)
                ],
                axis=0,
            )
        )
    top = stats[0]
    for s in range(1, n):
        top = jnp.maximum(top, stats[s])
    shares = []
    whole = jnp.zeros((rows, LANES), F32)
    for s in range(n):
        stat = stats[s]
        count = pltpu.roll(stat, LANES - heads, 1)
        share = jnp.exp2((stat - top) * EXPONENT) * count
        share = jnp.where(lane < heads, share, 0.0)
        shares.append(share)
        whole = whole + share
    inverse = 1.0 / jnp.where(lane < heads, whole, 1.0)
    shares = [share * inverse for share in shares]
    merged = [jnp.zeros((rows, HDIM), F32)] * heads
    for i in range(n):
        if i:
            o_copy(i, me).wait_recv()
        came = out_recv.at[source_of(i)] if i else out_send.at[me]
        for h in range(heads):
            part = slice(h * HDIM, (h + 1) * HDIM)
            merged[h] = merged[h] + shares[i][:, h : h + 1] * came[:, part].astype(F32)
    for h in range(heads):
        both_ref[1, :, h * HDIM : (h + 1) * HDIM] = merged[h].astype(BF16)

    for i in range(1, n):
        q_copy(i).wait_send()
        o_copy(i, me).wait_send()
        s_copy(i, me).wait_send()
        low = i & -i

        @pl.when(flipped(i - low) < flipped(low))
        def _(i=i):
            f_copy(i).wait_send()


def kernel_of_four(
    offset_ref,
    lengths_ref,
    streams_hbm,
    history_hbm,
    filters_hbm,
    skip_hbm,
    queries_hbm,
    kv_hbm,
    keys_hbm,
    values_hbm,
    both_ref,
    streams,
    history,
    filters,
    skip,
    queries,
    kv,
    keys,
    values,
    keys_across,
    history_wide,
    extended,
    toeplitz,
    all_q,
    out_send,
    out_recv,
    stat_send,
    stat_recv,
    carry_send,
    carry,
    in_sems,
    q_send,
    q_recv,
    f_send,
    f_recv,
    o_send,
    o_recv,
    s_send,
    s_recv,
    join,
):
    n = 4
    me = lax.axis_index("ctx")
    rows, channels = queries.shape
    heads = channels // HDIM
    groups, taps = filters.shape
    cache_rows = keys_hbm.shape[0]
    span = keys.shape[0]
    tile_groups = LANES // (channels // groups)
    chunk = heads // CHUNKS

    last = n - 1
    first = jnp.where(me == 0, 1, jnp.where(me == 1, 0, jnp.where(me == 2, 1, 2)))
    second = jnp.where(me < 2, 2, 0)
    third = jnp.where(me == last, 1, last)
    others = [first, second, third]

    barrier = pltpu.get_barrier_semaphore()

    @pl.when(me != last)
    def _():
        for i in range(1, n):
            pl.semaphore_signal(
                barrier,
                inc=1,
                device_id={"ctx": lax.rem(me + i, n)},
                device_id_type=MESH,
            )

    loads = [
        pltpu.make_async_copy(source, target, in_sems.at[i])
        for i, (source, target) in enumerate(
            [
                (queries_hbm, queries),
                (streams_hbm, streams),
                (kv_hbm, kv),
                (filters_hbm, filters),
                (history_hbm, history),
                (skip_hbm, skip),
                (keys_hbm, keys.at[pl.ds(0, cache_rows)]),
                (values_hbm, values.at[pl.ds(0, cache_rows)]),
            ]
        )
    ]
    for load in loads:
        load.start()

    position = (
        offset_ref[0] + me * rows + lax.broadcasted_iota(jnp.int32, (rows, HDIM), 0)
    ).astype(F32)
    lane = lax.broadcasted_iota(jnp.int32, (rows, HDIM), 1)
    pair = lax.broadcasted_iota(jnp.int32, (8, HDIM), 1) % (HDIM // 2)
    freq = jnp.ones((8, HDIM), F32)
    for i in range(1, HDIM // 2):
        freq = jnp.where(pair == i, float(1.0 / ROPE_BASE ** (2.0 * i / HDIM)), freq)
    cosine, sine = cos_sin(position * freq[0:1, :])
    sine = jnp.where(lane < HDIM // 2, -sine, sine)

    def rotated(x):
        x = x.astype(F32)
        return (x * cosine + pltpu.roll(x, HDIM // 2, 1) * sine).astype(BF16)

    def head(h):
        return slice(h * HDIM, (h + 1) * HDIM)

    loads[0].wait()
    for h in range(heads):
        all_q[me, h // chunk, :, head(h % chunk)] = rotated(queries[:, head(h)])

    def on(device, action):
        pl.when(me == device)(action)

    pl.semaphore_wait(barrier, jnp.where(me == last, n - 1, n - 2))

    @pl.when(me == last)
    def _():
        for i in range(n - 1):
            pl.semaphore_signal(
                join, inc=1, device_id={"ctx": i}, device_id_type=MESH
            )

    def q_copy(slot, block, target, c):
        return pltpu.make_async_remote_copy(
            src_ref=all_q.at[block, c],
            dst_ref=all_q.at[block, c],
            send_sem=q_send.at[slot, c],
            recv_sem=q_recv.at[block, c],
            device_id={"ctx": target},
            device_id_type=MESH,
        )

    def q_take(block, c):
        q_copy(0, block, lax.rem(me + 1, n), c).wait_recv()

    sent_q = [
        [(0, 2), (0, 1)],
        [(1, 2), (1, 0)],
        [(2, 0), (2, 1), (2, 3), (1, 3), (0, 3)],
        [(3, 0), (3, 1), (3, 2)],
    ]

    def q_starts(device, slots):
        for slot in slots:
            for c in range(CHUNKS):
                q_copy(slot, *sent_q[device][slot], c).start()

    for device in range(n):
        on(device, functools.partial(q_starts, device, (0, 1, 2) if device == 3 else (0, 1)))

    loads[1].wait()
    own_rows = pl.ds(pl.multiple_of(taps + me * rows, rows), rows)
    extended[own_rows, :] = (streams[1].astype(F32) * streams[2].astype(F32)).astype(BF16)

    passed = [(0, 1), (0, 2), (1, 2)]

    def f_copy(i):
        source, target = passed[i]
        block = extended.at[pl.ds(taps + source * rows, rows)]
        return pltpu.make_async_remote_copy(
            src_ref=block,
            dst_ref=block,
            send_sem=f_send.at[i],
            recv_sem=f_recv.at[i],
            device_id={"ctx": target},
            device_id_type=MESH,
        )

    def carry_copy():
        return pltpu.make_async_remote_copy(
            src_ref=carry_send,
            dst_ref=carry,
            send_sem=f_send.at[3],
            recv_sem=f_recv.at[3],
            device_id={"ctx": 3},
            device_id_type=MESH,
        )

    def f_starts():
        on(0, lambda: (f_copy(1).start(), f_copy(0).start(), None)[-1])
        on(1, lambda: f_copy(2).start())


    @pl.when(me == 3)
    def _():
        extended[taps : taps + 3 * rows, :] = jnp.zeros((3 * rows, channels), BF16)

    @pl.when(me != 3)
    def _():
        carry[...] = jnp.zeros((rows, channels), BF16)

    loads[2].wait()
    for h in range(heads):
        keys[pl.ds(cache_rows, rows), head(h)] = rotated(kv[0, :, head(h)])
    values[pl.ds(cache_rows, rows), :] = kv[1]
    pad = span - cache_rows - rows
    keys[pl.ds(cache_rows + rows, pad), :] = jnp.zeros((pad, channels), BF16)
    values[pl.ds(cache_rows + rows, pad), :] = jnp.zeros((pad, channels), BF16)

    @pl.when(me == 2)
    def _():
        pl.semaphore_wait(join, 1)
        q_starts(2, (2,))

    loads[3].wait()
    mirror = (
        lax.broadcasted_iota(jnp.int32, (taps, 2 * taps), 1)
        + lax.broadcasted_iota(jnp.int32, (taps, 2 * taps), 0)
        == taps
    ).astype(BF16)
    base = jnp.dot(filters[...], mirror, preferred_element_type=F32)
    for g in range(groups):
        line = jnp.broadcast_to(base[g : g + 1, :], (rows, 2 * taps))
        toeplitz[g * rows : (g + 1) * rows, :] = pltpu.roll(
            line, 0, 1, stride=1, stride_axis=0
        ).astype(BF16)

    loads[4].wait()
    history_wide[0:1, :] = jnp.zeros((1, channels), F32)
    history_wide[1:taps, :] = history[...].astype(F32)
    extended[0:taps, :] = history_wide[...].astype(BF16)
    loads[5].wait()

    loads[6].wait()
    for h in range(heads):
        keys_across[head(h), :] = keys[:, head(h)].T
    loads[7].wait()
    length = lengths_ref[0]
    cached = lax.broadcasted_iota(jnp.int32, (8, cache_rows), 1)
    cache_bias = jnp.where(cached < length, 0.0, MASKED)[0:1, :]
    block_column = lax.broadcasted_iota(jnp.int32, (rows, span - cache_rows), 1)
    block_token = lax.broadcasted_iota(jnp.int32, (rows, span - cache_rows), 0)

    def attend(source, mine, stat):
        kept = (block_column < rows) & (
            block_column + me * rows <= block_token + source * rows
        )
        block_bias = jnp.where(kept, 0.0, MASKED)
        scores = [
            jnp.dot(
                all_q[source, h // chunk, :, head(h % chunk)],
                keys_across[head(h), :],
                preferred_element_type=F32,
            )
            for h in mine
        ]
        scores = [
            jnp.concatenate(
                [score[:, :cache_rows] + cache_bias, score[:, cache_rows:] + block_bias],
                axis=1,
            )
            for score in scores
        ]
        tops = [jnp.max(score, axis=1, keepdims=True) for score in scores]
        weights = [
            jnp.exp2((score - top) * EXPONENT) for score, top in zip(scores, tops)
        ]
        totals = [jnp.sum(weight, axis=1, keepdims=True) for weight in weights]
        sums = [
            jnp.dot(weight.astype(BF16), values[:, head(h)], preferred_element_type=F32)
            for weight, h in zip(weights, mine)
        ]
        for i, h in enumerate(mine):
            out_send[source, h // chunk, :, head(h % chunk)] = (
                sums[i] / totals[i]
            ).astype(BF16)
            stat = jnp.where(lane == h, tops[i], stat)
            stat = jnp.where(lane == heads + h, totals[i], stat)
        return stat

    def packed(stat):
        result = stat[0:8]
        for a in range(1, rows // 8):
            result = result + pltpu.roll(stat[8 * a : 8 * a + 8], 2 * heads * a, 1)
        return result

    def o_copy(other, source, c):
        return pltpu.make_async_remote_copy(
            src_ref=out_send.at[other, c],
            dst_ref=out_recv.at[me, c],
            send_sem=o_send.at[other, c],
            recv_sem=o_recv.at[source, c],
            device_id={"ctx": other},
            device_id_type=MESH,
        )

    def s_copy(other, source):
        return pltpu.make_async_remote_copy(
            src_ref=stat_send.at[other],
            dst_ref=stat_recv.at[me],
            send_sem=s_send.at[other],
            recv_sem=s_recv.at[source],
            device_id={"ctx": other},
            device_id_type=MESH,
        )

    def conv_tile(j, window):
        stack = slice(j * tile_groups * rows, (j + 1) * tile_groups * rows)
        return jnp.dot(toeplitz[stack, 0:taps], window, preferred_element_type=F32)

    lane_group = lane // (channels // groups)

    def picked(product):
        conv = product[0:rows]
        for g in range(1, tile_groups):
            conv = jnp.where(lane_group == g, product[g * rows : (g + 1) * rows], conv)
        return conv

    def take_filter_inputs():
        on(1, lambda: f_copy(0).wait_recv())

        @pl.when(me == 2)
        def _():
            f_copy(1).wait_recv()
            f_copy(2).wait_recv()
            for j in range(channels // LANES):
                part = slice(j * LANES, (j + 1) * LANES)
                window = jnp.concatenate(
                    [
                        jnp.zeros((taps - 3 * rows, LANES), BF16),
                        extended[taps : taps + 3 * rows, part],
                    ],
                    axis=0,
                )
                carry_send[:, part] = picked(conv_tile(j, window)).astype(BF16)
            carry_copy().start()

    nothing = jnp.zeros((rows, LANES), F32)
    stat_send[me] = packed(attend(me, range(heads), nothing))

    def attend_and_send(other):
        stat_send[other] = packed(attend(other, range(heads), nothing))
        s_copy(other, me).start()
        for c in range(CHUNKS):
            o_copy(other, me, c).start()

    def take_all(block):
        for c in range(CHUNKS):
            q_take(block, c)

    def pass_on(device, slot):
        block = sent_q[device][slot][0]
        for c in range(CHUNKS):
            q_take(block, c)
            q_copy(slot, *sent_q[device][slot], c).start()

    @pl.when(me == 2)
    def _():
        pass_on(2, 4)
        pass_on(2, 3)

    @pl.when(me != 2)
    def _():
        take_all(first)

    f_starts()
    attend_and_send(first)
    pl.when(me != 2)(lambda: take_all(second))
    attend_and_send(second)
    take_filter_inputs()
    pl.when((me == 0) | (me == 1))(lambda: pl.semaphore_wait(join, 1))
    stat = nothing
    for c in range(CHUNKS):
        q_take(third, c)
        stat = attend(third, range(c * chunk, (c + 1) * chunk), stat)
        if c == CHUNKS - 1:
            stat_send[third] = packed(stat)
            s_copy(third, me).start()
        o_copy(third, me, c).start()

    on(3, lambda: carry_copy().wait_recv())
    direct = skip[...].astype(F32).reshape(1, channels)
    for j in range(channels // LANES):
        part = slice(j * LANES, (j + 1) * LANES)
        stack = slice(j * tile_groups * rows, (j + 1) * tile_groups * rows)
        mine = extended[own_rows, part]
        window = extended[pl.ds(pl.multiple_of(me * rows, rows), taps), part]
        product = conv_tile(j, window) + jnp.dot(
            toeplitz[stack, taps : taps + rows], mine, preferred_element_type=F32
        )
        conv = picked(product) + carry[:, part].astype(F32)
        both_ref[0, :, part] = (
            streams[0, :, part].astype(F32)
            * (conv + direct[:, part] * mine.astype(F32))
        ).astype(BF16)

    for other in others:
        s_copy(other, other).wait_recv()

    def unpacked(value):
        return jnp.concatenate(
            [value]
            + [
                pltpu.roll(value, LANES - 2 * heads * a, 1) for a in range(1, rows // 8)
            ],
            axis=0,
        )

    came = [unpacked(stat_send[me])] + [unpacked(stat_recv[other]) for other in others]
    top = came[0]
    for stat in came[1:]:
        top = jnp.maximum(top, stat)
    shares = []
    whole = jnp.zeros((rows, LANES), F32)
    for stat in came:
        count = pltpu.roll(stat, LANES - heads, 1)
        share = jnp.exp2((stat - top) * EXPONENT) * count
        share = jnp.where(lane < heads, share, 0.0)
        shares.append(share)
        whole = whole + share
    inverse = 1.0 / jnp.where(lane < heads, whole, 1.0)
    shares = [share * inverse for share in shares]
    merged = [
        shares[0][:, h : h + 1]
        * out_send[me, h // chunk, :, head(h % chunk)].astype(F32)
        for h in range(heads)
    ]
    for kind in (0, 1, 2):
        for c in range(CHUNKS):
            o_copy(others[kind], others[kind], c).wait_recv()
            for h in range(c * chunk, (c + 1) * chunk):
                merged[h] = merged[h] + shares[kind + 1][:, h : h + 1] * out_recv[
                    others[kind], c, :, head(h - c * chunk)
                ].astype(F32)
    for h in range(heads):
        both_ref[1, :, head(h)] = merged[h].astype(BF16)

    for other in others:
        for c in range(CHUNKS):
            o_copy(other, me, c).wait_send()
        s_copy(other, me).wait_send()

    def q_ends(device):
        for slot in range(len(sent_q[device])):
            for c in range(CHUNKS):
                q_copy(slot, *sent_q[device][slot], c).wait_send()

    for device in range(n):
        on(device, functools.partial(q_ends, device))
    on(0, lambda: (f_copy(0).wait_send(), f_copy(1).wait_send(), None)[-1])
    on(1, lambda: f_copy(2).wait_send())
    on(2, lambda: carry_copy().wait_send())


def four_shards(
    streams,
    history,
    filters,
    skip_weight,
    offset,
    lengths,
    queries,
    block_kv,
    cache_keys,
    cache_values,
):
    n = 4
    rows, channels = queries.shape
    groups, taps = filters.shape
    cache_rows = cache_keys.shape[0]
    span = cache_rows + LANES
    wide = channels // CHUNKS
    any_space = pl.BlockSpec(memory_space=pl.ANY)
    smem = pl.BlockSpec(memory_space=pltpu.SMEM)
    vmem = pl.BlockSpec(memory_space=pltpu.VMEM)
    dma = pltpu.SemaphoreType.DMA
    in_hbm = [
        pltpu.with_memory_space_constraint(x, pltpu.HBM)
        for x in (
            streams,
            history,
            filters,
            skip_weight,
            queries,
            block_kv,
            cache_keys,
            cache_values,
        )
    ]
    both = pl.pallas_call(
        kernel_of_four,
        out_shape=jax.ShapeDtypeStruct((2, rows, channels), BF16),
        in_specs=[smem, smem] + [any_space] * 8,
        out_specs=vmem,
        scratch_shapes=[
            pltpu.VMEM(streams.shape, BF16),
            pltpu.VMEM(history.shape, BF16),
            pltpu.VMEM(filters.shape, BF16),
            pltpu.VMEM((channels,), BF16),
            pltpu.VMEM((rows, channels), BF16),
            pltpu.VMEM(block_kv.shape, BF16),
            pltpu.VMEM((span, channels), BF16),
            pltpu.VMEM((span, channels), BF16),
            pltpu.VMEM((channels, span), BF16),
            pltpu.VMEM((taps, channels), F32),
            pltpu.VMEM((taps + n * rows, channels), BF16),
            pltpu.VMEM((groups * rows, 2 * taps), BF16),
            pltpu.VMEM((n, CHUNKS, rows, wide), BF16),
            pltpu.VMEM((n, CHUNKS, rows, wide), BF16),
            pltpu.VMEM((n, CHUNKS, rows, wide), BF16),
            pltpu.VMEM((n, 8, LANES), F32),
            pltpu.VMEM((n, 8, LANES), F32),
            pltpu.VMEM((rows, channels), BF16),
            pltpu.VMEM((rows, channels), BF16),
            dma((8,)),
            dma((5, CHUNKS)),
            dma((n, CHUNKS)),
            dma((4,)),
            dma((4,)),
            dma((n, CHUNKS)),
            dma((n, CHUNKS)),
            dma((n,)),
            dma((n,)),
            pltpu.SemaphoreType.REGULAR,
        ],
        compiler_params=pltpu.CompilerParams(
            collective_id=0, has_side_effects=True, vmem_limit_bytes=VMEM_LIMIT
        ),
    )(
        offset,
        lengths,
        *in_hbm,
    )
    return both[0], both[1]


def shards(
    n,
    streams,
    history,
    filters,
    skip_weight,
    offset,
    lengths,
    queries,
    block_kv,
    cache_keys,
    cache_values,
):
    rows, channels = queries.shape
    groups, taps = filters.shape
    cache_rows = cache_keys.shape[0]
    span = cache_rows + LANES
    if n == 4:
        return four_shards(
            streams,
            history,
            filters,
            skip_weight,
            offset,
            lengths,
            queries,
            block_kv,
            cache_keys,
            cache_values,
        )
    any_space = pl.BlockSpec(memory_space=pl.ANY)
    smem = pl.BlockSpec(memory_space=pltpu.SMEM)
    vmem = pl.BlockSpec(memory_space=pltpu.VMEM)
    dma = pltpu.SemaphoreType.DMA
    in_hbm = [
        pltpu.with_memory_space_constraint(x, pltpu.HBM)
        for x in (
            streams,
            history,
            filters,
            skip_weight,
            queries,
            block_kv,
            cache_keys,
            cache_values,
        )
    ]
    both = pl.pallas_call(
        functools.partial(kernel, n),
        out_shape=jax.ShapeDtypeStruct((2, rows, channels), BF16),
        in_specs=[smem, smem] + [any_space] * 8,
        out_specs=vmem,
        scratch_shapes=[
            pltpu.VMEM(streams.shape, BF16),
            pltpu.VMEM(history.shape, BF16),
            pltpu.VMEM(filters.shape, BF16),
            pltpu.VMEM((channels,), BF16),
            pltpu.VMEM((rows, channels), BF16),
            pltpu.VMEM(block_kv.shape, BF16),
            pltpu.VMEM((span, channels), BF16),
            pltpu.VMEM((span, channels), BF16),
            pltpu.VMEM((taps, channels), F32),
            pltpu.VMEM((taps + n * rows, channels), BF16),
            pltpu.VMEM((groups * rows, 2 * taps), BF16),
            pltpu.VMEM((n, rows, channels), BF16),
            pltpu.VMEM((n, rows, channels), BF16),
            pltpu.VMEM((n, rows, channels), BF16),
            pltpu.VMEM((n, 8, LANES), F32),
            pltpu.VMEM((n, 8, LANES), F32),
            dma((8,)),
            dma((n,)),
            dma((n,)),
            dma((n,)),
            dma((n,)),
            dma((n,)),
            dma((n,)),
            dma((n,)),
            dma((n,)),
        ],
        compiler_params=pltpu.CompilerParams(
            collective_id=0, has_side_effects=True, vmem_limit_bytes=VMEM_LIMIT
        ),
    )(
        offset,
        lengths,
        *in_hbm,
    )
    return both[0], both[1]


def solution(mesh):
    return jax.shard_map(
        functools.partial(shards, mesh.shape["ctx"]),
        mesh=mesh,
        in_specs=(
            P(None, ("seqs", "ctx"), ("head", "sub")),
            P("seqs", ("head", "sub")),
            P(("head", "sub"), None),
            P(("head", "sub")),
            P("seqs"),
            P(("seqs", "ctx")),
            P(("seqs", "ctx"), ("head", "sub")),
            P(None, ("seqs", "ctx"), ("head", "sub")),
            P(("seqs", "ctx"), ("head", "sub")),
            P(("seqs", "ctx"), ("head", "sub")),
        ),
        out_specs=(P(("seqs", "ctx"), ("head", "sub")), P(("seqs", "ctx"), ("head", "sub"))),
        check_vma=False,
    )
```

```python
import functools
import math

import jax
import jax.numpy as jnp
from jax import lax
from jax.experimental import pallas as pl
from jax.experimental.pallas import tpu as pltpu
from jax.sharding import PartitionSpec as P

HDIM = 128
ROPE_BASE = 1000000.0
MASKED = -1e30
MESH = pl.DeviceIdType.MESH
F32 = jnp.float32
BF16 = jnp.bfloat16
LANES = 128
CHUNKS = 2
VMEM_LIMIT = 32 * 2**20
EXPONENT = math.log2(math.e) / math.sqrt(HDIM)


def cos_sin(x):
    quarter = jnp.floor(x * (2.0 / math.pi) + 0.5)
    r = x - quarter * 1.5703125
    r = r - quarter * 4.837512969970703125e-4
    r = r - quarter * 7.54978995489188216e-8
    z = r * r
    sine = ((-1.9515295891e-4 * z + 8.3321608736e-3) * z - 1.6666654611e-1) * z * r + r
    cosine = (
        ((2.443315711809948e-5 * z - 1.388731625493765e-3) * z + 4.166664568298827e-2) * z * z
        - 0.5 * z
        + 1.0
    )
    turn = quarter.astype(jnp.int32) & 3
    odd = (turn & 1) == 1
    cos_x = jnp.where(odd, sine, cosine)
    sin_x = jnp.where(odd, cosine, sine)
    cos_x = jnp.where((turn == 1) | (turn == 2), -cos_x, cos_x)
    sin_x = jnp.where(turn >= 2, -sin_x, sin_x)
    return cos_x, sin_x


def kernel(
    n,
    offset_ref,
    lengths_ref,
    streams_hbm,
    history_hbm,
    filters_hbm,
    skip_hbm,
    queries_hbm,
    kv_hbm,
    keys_hbm,
    values_hbm,
    both_ref,
    streams,
    history,
    filters,
    skip,
    queries,
    kv,
    keys,
    values,
    history_wide,
    extended,
    toeplitz,
    all_q,
    out_send,
    out_recv,
    stat_send,
    stat_recv,
    in_sems,
    q_send,
    q_recv,
    f_send,
    f_recv,
    o_send,
    o_recv,
    s_send,
    s_recv,
):
    me = lax.axis_index("ctx")
    rows, channels = queries.shape
    heads = channels // HDIM
    groups, taps = filters.shape
    cache_rows = keys_hbm.shape[0]
    span = keys.shape[0]
    tile_groups = LANES // (channels // groups)

    barrier = pltpu.get_barrier_semaphore()
    for i in range(1, n):
        pl.semaphore_signal(
            barrier, inc=1, device_id={"ctx": lax.rem(me + i, n)}, device_id_type=MESH
        )

    loads = [
        pltpu.make_async_copy(source, target, in_sems.at[i])
        for i, (source, target) in enumerate(
            [
                (queries_hbm, queries),
                (streams_hbm, streams),
                (kv_hbm, kv),
                (filters_hbm, filters),
                (history_hbm, history),
                (skip_hbm, skip),
                (keys_hbm, keys.at[pl.ds(0, cache_rows)]),
                (values_hbm, values.at[pl.ds(0, cache_rows)]),
            ]
        )
    ]
    for load in loads:
        load.start()

    position = (
        offset_ref[0] + me * rows + lax.broadcasted_iota(jnp.int32, (rows, HDIM), 0)
    ).astype(F32)
    lane = lax.broadcasted_iota(jnp.int32, (rows, HDIM), 1)
    pair = lax.broadcasted_iota(jnp.int32, (8, HDIM), 1) % (HDIM // 2)
    freq = jnp.ones((8, HDIM), F32)
    for i in range(1, HDIM // 2):
        freq = jnp.where(pair == i, float(1.0 / ROPE_BASE ** (2.0 * i / HDIM)), freq)
    cosine, sine = cos_sin(position * freq[0:1, :])
    sine = jnp.where(lane < HDIM // 2, -sine, sine)

    def rotated(x):
        x = x.astype(F32)
        return (x * cosine + pltpu.roll(x, HDIM // 2, 1) * sine).astype(BF16)

    loads[0].wait()
    for h in range(heads):
        part = slice(h * HDIM, (h + 1) * HDIM)
        all_q[me, :, part] = rotated(queries[:, part])

    pl.semaphore_wait(barrier, n - 1)

    def flipped(i):
        result = me
        for b in [1 << k for k in range(n.bit_length()) if i >> k & 1]:
            result = result + b * (1 - 2 * lax.rem(lax.div(me, b), 2))
        return result

    def children(i):
        low = i & -i if i else n
        return [i + (1 << k) for k in reversed(range(n.bit_length())) if (1 << k) < low]

    def q_copy(i):
        low = i & -i
        block = flipped(i - low)
        return pltpu.make_async_remote_copy(
            src_ref=all_q.at[block],
            dst_ref=all_q.at[block],
            send_sem=q_send.at[i],
            recv_sem=q_recv.at[i],
            device_id={"ctx": flipped(low)},
            device_id_type=MESH,
        )

    for i in children(0):
        q_copy(i).start()

    loads[1].wait()
    own_rows = pl.ds(pl.multiple_of(taps + me * rows, rows), rows)
    extended[own_rows, :] = (streams[1].astype(F32) * streams[2].astype(F32)).astype(BF16)

    def f_copy(i):
        low = i & -i
        start = pl.multiple_of(taps + flipped(i - low) * rows, rows)
        return pltpu.make_async_remote_copy(
            src_ref=extended.at[pl.ds(start, rows)],
            dst_ref=extended.at[pl.ds(start, rows)],
            send_sem=f_send.at[i],
            recv_sem=f_recv.at[i],
            device_id={"ctx": flipped(low)},
            device_id_type=MESH,
        )

    def f_start(i):
        low = i & -i

        @pl.when(flipped(i - low) < flipped(low))
        def _():
            f_copy(i).start()

    def f_take(i):
        @pl.when(flipped(i) < me)
        def _():
            f_copy(i).wait_recv()

        for j in children(i):
            f_start(j)

    def q_take(i):
        q_copy(i).wait_recv()
        for j in children(i):
            q_copy(j).start()

    for i in children(0):
        f_start(i)

    loads[2].wait()
    for h in range(heads):
        part = slice(h * HDIM, (h + 1) * HDIM)
        keys[pl.ds(cache_rows, rows), part] = rotated(kv[0, :, part])
    values[pl.ds(cache_rows, rows), :] = kv[1]
    pad = span - cache_rows - rows
    keys[pl.ds(cache_rows + rows, pad), :] = jnp.zeros((pad, channels), BF16)
    values[pl.ds(cache_rows + rows, pad), :] = jnp.zeros((pad, channels), BF16)

    loads[3].wait()
    mirror = (
        lax.broadcasted_iota(jnp.int32, (taps, 2 * taps), 1)
        + lax.broadcasted_iota(jnp.int32, (taps, 2 * taps), 0)
        == taps
    ).astype(BF16)
    base = jnp.dot(filters[...], mirror, preferred_element_type=F32)
    for g in range(groups):
        line = jnp.broadcast_to(base[g : g + 1, :], (rows, 2 * taps))
        toeplitz[g * rows : (g + 1) * rows, :] = pltpu.roll(
            line, 0, 1, stride=1, stride_axis=0
        ).astype(BF16)

    loads[4].wait()
    history_wide[0:1, :] = jnp.zeros((1, channels), F32)
    history_wide[1:taps, :] = history[...].astype(F32)
    extended[0:taps, :] = history_wide[...].astype(BF16)
    loads[5].wait()

    loads[6].wait()
    loads[7].wait()
    column = lax.broadcasted_iota(jnp.int32, (rows, span), 1)
    token = lax.broadcasted_iota(jnp.int32, (rows, span), 0)
    length = lengths_ref[0]

    def attend(source):
        kept = (column < jnp.minimum(length, cache_rows)) | (
            (column >= cache_rows)
            & (column < cache_rows + rows)
            & (column - cache_rows + me * rows <= token + source * rows)
        )
        bias = jnp.where(kept, 0.0, MASKED)
        stat = jnp.zeros((rows, LANES), F32)
        parts = [slice(h * HDIM, (h + 1) * HDIM) for h in range(heads)]
        scores = [
            lax.dot_general(
                all_q[source, :, part],
                keys[:, part],
                (((1,), (1,)), ((), ())),
                preferred_element_type=F32,
            )
            + bias
            for part in parts
        ]
        tops = [jnp.max(score, axis=1, keepdims=True) for score in scores]
        weights = [
            jnp.exp2((score - top) * EXPONENT) for score, top in zip(scores, tops)
        ]
        totals = [jnp.sum(weight, axis=1, keepdims=True) for weight in weights]
        sums = [
            jnp.dot(weight.astype(BF16), values[:, part], preferred_element_type=F32)
            for weight, part in zip(weights, parts)
        ]
        for h in range(heads):
            out_send[source, :, parts[h]] = (sums[h] / totals[h]).astype(BF16)
            stat = jnp.where(lane == h, tops[h], stat)
            stat = jnp.where(lane == heads + h, totals[h], stat)
        packed = stat[0:8]
        for a in range(1, rows // 8):
            packed = packed + pltpu.roll(stat[8 * a : 8 * a + 8], 2 * heads * a, 1)
        stat_send[source] = packed

    def o_copy(i, source):
        return pltpu.make_async_remote_copy(
            src_ref=out_send.at[source],
            dst_ref=out_recv.at[me],
            send_sem=o_send.at[i],
            recv_sem=o_recv.at[i],
            device_id={"ctx": source},
            device_id_type=MESH,
        )

    def s_copy(i, source):
        return pltpu.make_async_remote_copy(
            src_ref=stat_send.at[source],
            dst_ref=stat_recv.at[me],
            send_sem=s_send.at[i],
            recv_sem=s_recv.at[i],
            device_id={"ctx": source},
            device_id_type=MESH,
        )

    def attend_and_send(i, source):
        attend(source)
        s_copy(i, source).start()
        o_copy(i, source).start()

    attend(me)
    if n == 4:
        q_take(2)
        q_take(1)
        attend_and_send(1, flipped(1))
        f_take(2)
        attend_and_send(2, flipped(2))
        q_take(3)
        attend_and_send(3, flipped(3))
        f_take(1)
        f_take(3)
    else:
        for i in sorted(range(1, n), key=lambda i: i.bit_count()):
            q_take(i)
            f_take(i)

        def step(i, _):
            attend_and_send(i, lax.rem(me - i + n, n))
            return 0

        lax.fori_loop(1, n, step, 0)

    direct = skip[...].astype(F32).reshape(1, channels)
    lane_group = lane // (channels // groups)
    for j in range(channels // LANES):
        part = slice(j * LANES, (j + 1) * LANES)
        stack = slice(j * tile_groups * rows, (j + 1) * tile_groups * rows)
        own = extended[own_rows, part]
        window = extended[pl.ds(pl.multiple_of(me * rows, rows), taps), part]
        product = jnp.dot(
            toeplitz[stack, 0:taps], window, preferred_element_type=F32
        ) + jnp.dot(toeplitz[stack, taps : taps + rows], own, preferred_element_type=F32)
        conv = product[0:rows]
        for g in range(1, tile_groups):
            conv = jnp.where(lane_group == g, product[g * rows : (g + 1) * rows], conv)
        both_ref[0, :, part] = (
            streams[0, :, part].astype(F32)
            * (conv + direct[:, part] * own.astype(F32))
        ).astype(BF16)

    for i in range(1, n):
        s_copy(i, me).wait_recv()

    stat_recv[me] = stat_send[me]
    def source_of(i):
        return flipped(i) if n == 4 else lax.rem(me + i, n)

    stats = []
    for i in range(n):
        packed = stat_recv[source_of(i)]
        stats.append(
            jnp.concatenate(
                [packed]
                + [
                    pltpu.roll(packed, LANES - 2 * heads * a, 1)
                    for a in range(1, rows // 8)
                ],
                axis=0,
            )
        )
    top = stats[0]
    for s in range(1, n):
        top = jnp.maximum(top, stats[s])
    shares = []
    whole = jnp.zeros((rows, LANES), F32)
    for s in range(n):
        stat = stats[s]
        count = pltpu.roll(stat, LANES - heads, 1)
        share = jnp.exp2((stat - top) * EXPONENT) * count
        share = jnp.where(lane < heads, share, 0.0)
        shares.append(share)
        whole = whole + share
    inverse = 1.0 / jnp.where(lane < heads, whole, 1.0)
    shares = [share * inverse for share in shares]
    merged = [jnp.zeros((rows, HDIM), F32)] * heads
    for i in range(n):
        if i:
            o_copy(i, me).wait_recv()
        came = out_recv.at[source_of(i)] if i else out_send.at[me]
        for h in range(heads):
            part = slice(h * HDIM, (h + 1) * HDIM)
            merged[h] = merged[h] + shares[i][:, h : h + 1] * came[:, part].astype(F32)
    for h in range(heads):
        both_ref[1, :, h * HDIM : (h + 1) * HDIM] = merged[h].astype(BF16)

    for i in range(1, n):
        q_copy(i).wait_send()
        o_copy(i, me).wait_send()
        s_copy(i, me).wait_send()
        low = i & -i

        @pl.when(flipped(i - low) < flipped(low))
        def _(i=i):
            f_copy(i).wait_send()


def kernel_of_four(
    offset_ref,
    lengths_ref,
    streams_hbm,
    history_hbm,
    filters_hbm,
    skip_hbm,
    queries_hbm,
    kv_hbm,
    keys_hbm,
    values_hbm,
    both_ref,
    streams,
    history,
    filters,
    skip,
    queries,
    kv,
    keys,
    values,
    keys_across,
    history_wide,
    extended,
    toeplitz,
    all_q,
    out_send,
    out_recv,
    stat_send,
    stat_recv,
    carry_send,
    carry,
    in_sems,
    q_send,
    q_recv,
    f_send,
    f_recv,
    o_send,
    o_recv,
    s_send,
    s_recv,
    join,
):
    n = 4
    me = lax.axis_index("ctx")
    rows, channels = queries.shape
    heads = channels // HDIM
    groups, taps = filters.shape
    cache_rows = keys_hbm.shape[0]
    span = keys.shape[0]
    tile_groups = LANES // (channels // groups)
    chunk = heads // CHUNKS

    last = n - 1
    first = jnp.where(me == 0, 1, jnp.where(me == 1, 0, jnp.where(me == 2, 1, 2)))
    second = jnp.where(me < 2, 2, 0)
    third = jnp.where(me == last, 1, last)
    others = [first, second, third]

    barrier = pltpu.get_barrier_semaphore()

    @pl.when(me != last)
    def _():
        for i in range(1, n):
            pl.semaphore_signal(
                barrier,
                inc=1,
                device_id={"ctx": lax.rem(me + i, n)},
                device_id_type=MESH,
            )

    loads = [
        pltpu.make_async_copy(source, target, in_sems.at[i])
        for i, (source, target) in enumerate(
            [
                (queries_hbm, queries),
                (streams_hbm, streams),
                (kv_hbm, kv),
                (filters_hbm, filters),
                (history_hbm, history),
                (skip_hbm, skip),
                (keys_hbm, keys.at[pl.ds(0, cache_rows)]),
                (values_hbm, values.at[pl.ds(0, cache_rows)]),
            ]
        )
    ]
    for load in loads:
        load.start()

    position = (
        offset_ref[0] + me * rows + lax.broadcasted_iota(jnp.int32, (rows, HDIM), 0)
    ).astype(F32)
    lane = lax.broadcasted_iota(jnp.int32, (rows, HDIM), 1)
    pair = lax.broadcasted_iota(jnp.int32, (8, HDIM), 1) % (HDIM // 2)
    freq = jnp.ones((8, HDIM), F32)
    for i in range(1, HDIM // 2):
        freq = jnp.where(pair == i, float(1.0 / ROPE_BASE ** (2.0 * i / HDIM)), freq)
    cosine, sine = cos_sin(position * freq[0:1, :])
    sine = jnp.where(lane < HDIM // 2, -sine, sine)

    def rotated(x):
        x = x.astype(F32)
        return (x * cosine + pltpu.roll(x, HDIM // 2, 1) * sine).astype(BF16)

    def head(h):
        return slice(h * HDIM, (h + 1) * HDIM)

    loads[0].wait()
    for h in range(heads):
        all_q[me, h // chunk, :, head(h % chunk)] = rotated(queries[:, head(h)])

    def on(device, action):
        pl.when(me == device)(action)

    pl.semaphore_wait(barrier, jnp.where(me == last, n - 1, n - 2))

    @pl.when(me == last)
    def _():
        for i in range(n - 1):
            pl.semaphore_signal(
                join, inc=1, device_id={"ctx": i}, device_id_type=MESH
            )

    def q_copy(slot, block, target, c):
        return pltpu.make_async_remote_copy(
            src_ref=all_q.at[block, c],
            dst_ref=all_q.at[block, c],
            send_sem=q_send.at[slot, c],
            recv_sem=q_recv.at[block, c],
            device_id={"ctx": target},
            device_id_type=MESH,
        )

    def q_take(block, c):
        q_copy(0, block, lax.rem(me + 1, n), c).wait_recv()

    sent_q = [
        [(0, 2), (0, 1), (0, 3)],
        [(1, 2), (1, 0)],
        [(2, 0), (2, 1), (2, 3), (1, 3)],
        [(3, 0), (3, 1), (3, 2)],
    ]

    def q_starts(device, slots):
        for slot in slots:
            for c in range(CHUNKS):
                q_copy(slot, *sent_q[device][slot], c).start()

    for device in range(n):
        on(device, functools.partial(q_starts, device, (0, 1, 2) if device == 3 else (0, 1)))

    loads[1].wait()
    own_rows = pl.ds(pl.multiple_of(taps + me * rows, rows), rows)
    extended[own_rows, :] = (streams[1].astype(F32) * streams[2].astype(F32)).astype(BF16)

    passed = [(0, 1), (0, 2), (1, 2)]

    def f_copy(i):
        source, target = passed[i]
        block = extended.at[pl.ds(taps + source * rows, rows)]
        return pltpu.make_async_remote_copy(
            src_ref=block,
            dst_ref=block,
            send_sem=f_send.at[i],
            recv_sem=f_recv.at[i],
            device_id={"ctx": target},
            device_id_type=MESH,
        )

    def carry_copy():
        return pltpu.make_async_remote_copy(
            src_ref=carry_send,
            dst_ref=carry,
            send_sem=f_send.at[3],
            recv_sem=f_recv.at[3],
            device_id={"ctx": 3},
            device_id_type=MESH,
        )

    def f_starts():
        on(0, lambda: (f_copy(1).start(), f_copy(0).start(), None)[-1])
        on(1, lambda: f_copy(2).start())


    @pl.when(me == 3)
    def _():
        extended[taps : taps + 3 * rows, :] = jnp.zeros((3 * rows, channels), BF16)

    @pl.when(me != 3)
    def _():
        carry[...] = jnp.zeros((rows, channels), BF16)

    loads[2].wait()
    for h in range(heads):
        keys[pl.ds(cache_rows, rows), head(h)] = rotated(kv[0, :, head(h)])
    values[pl.ds(cache_rows, rows), :] = kv[1]
    pad = span - cache_rows - rows
    keys[pl.ds(cache_rows + rows, pad), :] = jnp.zeros((pad, channels), BF16)
    values[pl.ds(cache_rows + rows, pad), :] = jnp.zeros((pad, channels), BF16)

    @pl.when(me == 2)
    def _():
        pl.semaphore_wait(join, 1)
        q_starts(2, (2,))

    loads[3].wait()
    mirror = (
        lax.broadcasted_iota(jnp.int32, (taps, 2 * taps), 1)
        + lax.broadcasted_iota(jnp.int32, (taps, 2 * taps), 0)
        == taps
    ).astype(BF16)
    base = jnp.dot(filters[...], mirror, preferred_element_type=F32)
    for g in range(groups):
        line = jnp.broadcast_to(base[g : g + 1, :], (rows, 2 * taps))
        toeplitz[g * rows : (g + 1) * rows, :] = pltpu.roll(
            line, 0, 1, stride=1, stride_axis=0
        ).astype(BF16)

    loads[4].wait()
    history_wide[0:1, :] = jnp.zeros((1, channels), F32)
    history_wide[1:taps, :] = history[...].astype(F32)
    extended[0:taps, :] = history_wide[...].astype(BF16)
    loads[5].wait()

    loads[6].wait()
    for h in range(heads):
        keys_across[head(h), :] = keys[:, head(h)].T
    loads[7].wait()
    length = lengths_ref[0]
    cached = lax.broadcasted_iota(jnp.int32, (8, cache_rows), 1)
    cache_bias = jnp.where(cached < length, 0.0, MASKED)[0:1, :]
    block_column = lax.broadcasted_iota(jnp.int32, (rows, span - cache_rows), 1)
    block_token = lax.broadcasted_iota(jnp.int32, (rows, span - cache_rows), 0)

    def attend(source, mine, stat):
        kept = (block_column < rows) & (
            block_column + me * rows <= block_token + source * rows
        )
        block_bias = jnp.where(kept, 0.0, MASKED)
        scores = [
            jnp.dot(
                all_q[source, h // chunk, :, head(h % chunk)],
                keys_across[head(h), :],
                preferred_element_type=F32,
            )
            for h in mine
        ]
        scores = [
            jnp.concatenate(
                [score[:, :cache_rows] + cache_bias, score[:, cache_rows:] + block_bias],
                axis=1,
            )
            for score in scores
        ]
        tops = [jnp.max(score, axis=1, keepdims=True) for score in scores]
        weights = [
            jnp.exp2((score - top) * EXPONENT) for score, top in zip(scores, tops)
        ]
        totals = [jnp.sum(weight, axis=1, keepdims=True) for weight in weights]
        sums = [
            jnp.dot(weight.astype(BF16), values[:, head(h)], preferred_element_type=F32)
            for weight, h in zip(weights, mine)
        ]
        for i, h in enumerate(mine):
            out_send[source, h // chunk, :, head(h % chunk)] = (
                sums[i] / totals[i]
            ).astype(BF16)
            stat = jnp.where(lane == h, tops[i], stat)
            stat = jnp.where(lane == heads + h, totals[i], stat)
        return stat

    def packed(stat):
        result = stat[0:8]
        for a in range(1, rows // 8):
            result = result + pltpu.roll(stat[8 * a : 8 * a + 8], 2 * heads * a, 1)
        return result

    def o_copy(other, source, c):
        return pltpu.make_async_remote_copy(
            src_ref=out_send.at[other, c],
            dst_ref=out_recv.at[me, c],
            send_sem=o_send.at[other, c],
            recv_sem=o_recv.at[source, c],
            device_id={"ctx": other},
            device_id_type=MESH,
        )

    def s_copy(other, source):
        return pltpu.make_async_remote_copy(
            src_ref=stat_send.at[other],
            dst_ref=stat_recv.at[me],
            send_sem=s_send.at[other],
            recv_sem=s_recv.at[source],
            device_id={"ctx": other},
            device_id_type=MESH,
        )

    def conv_tile(j, window):
        stack = slice(j * tile_groups * rows, (j + 1) * tile_groups * rows)
        return jnp.dot(toeplitz[stack, 0:taps], window, preferred_element_type=F32)

    lane_group = lane // (channels // groups)

    def picked(product):
        conv = product[0:rows]
        for g in range(1, tile_groups):
            conv = jnp.where(lane_group == g, product[g * rows : (g + 1) * rows], conv)
        return conv

    def take_filter_inputs():
        on(1, lambda: f_copy(0).wait_recv())

        @pl.when(me == 2)
        def _():
            f_copy(1).wait_recv()
            f_copy(2).wait_recv()
            for j in range(channels // LANES):
                part = slice(j * LANES, (j + 1) * LANES)
                window = jnp.concatenate(
                    [
                        jnp.zeros((taps - 3 * rows, LANES), BF16),
                        extended[taps : taps + 3 * rows, part],
                    ],
                    axis=0,
                )
                carry_send[:, part] = picked(conv_tile(j, window)).astype(BF16)
            carry_copy().start()

    nothing = jnp.zeros((rows, LANES), F32)
    def attend_and_send(other):
        stat_send[other] = packed(attend(other, range(heads), nothing))
        s_copy(other, me).start()
        for c in range(CHUNKS):
            o_copy(other, me, c).start()

    def take_all(block):
        for c in range(CHUNKS):
            q_take(block, c)

    def pass_on(device, slot):
        block = sent_q[device][slot][0]
        for c in range(CHUNKS):
            q_take(block, c)
            q_copy(slot, *sent_q[device][slot], c).start()

    @pl.when(me == 0)
    def _():
        pl.semaphore_wait(join, 1)
        q_starts(0, (2,))

    stat_send[me] = packed(attend(me, range(heads), nothing))

    on(2, lambda: pass_on(2, 3))

    @pl.when(me != 2)
    def _():
        take_all(first)

    f_starts()
    attend_and_send(first)
    take_all(second)
    attend_and_send(second)
    take_filter_inputs()
    on(1, lambda: pl.semaphore_wait(join, 1))
    stat = nothing
    for c in range(CHUNKS):
        q_take(third, c)
        stat = attend(third, range(c * chunk, (c + 1) * chunk), stat)
        if c == CHUNKS - 1:
            stat_send[third] = packed(stat)
            s_copy(third, me).start()
        o_copy(third, me, c).start()

    on(3, lambda: carry_copy().wait_recv())
    direct = skip[...].astype(F32).reshape(1, channels)
    for j in range(channels // LANES):
        part = slice(j * LANES, (j + 1) * LANES)
        stack = slice(j * tile_groups * rows, (j + 1) * tile_groups * rows)
        mine = extended[own_rows, part]
        window = extended[pl.ds(pl.multiple_of(me * rows, rows), taps), part]
        product = conv_tile(j, window) + jnp.dot(
            toeplitz[stack, taps : taps + rows], mine, preferred_element_type=F32
        )
        conv = picked(product) + carry[:, part].astype(F32)
        both_ref[0, :, part] = (
            streams[0, :, part].astype(F32)
            * (conv + direct[:, part] * mine.astype(F32))
        ).astype(BF16)

    for other in others:
        s_copy(other, other).wait_recv()

    def unpacked(value):
        return jnp.concatenate(
            [value]
            + [
                pltpu.roll(value, LANES - 2 * heads * a, 1) for a in range(1, rows // 8)
            ],
            axis=0,
        )

    came = [unpacked(stat_send[me])] + [unpacked(stat_recv[other]) for other in others]
    top = came[0]
    for stat in came[1:]:
        top = jnp.maximum(top, stat)
    shares = []
    whole = jnp.zeros((rows, LANES), F32)
    for stat in came:
        count = pltpu.roll(stat, LANES - heads, 1)
        share = jnp.exp2((stat - top) * EXPONENT) * count
        share = jnp.where(lane < heads, share, 0.0)
        shares.append(share)
        whole = whole + share
    inverse = 1.0 / jnp.where(lane < heads, whole, 1.0)
    shares = [share * inverse for share in shares]
    merged = [
        shares[0][:, h : h + 1]
        * out_send[me, h // chunk, :, head(h % chunk)].astype(F32)
        for h in range(heads)
    ]
    for kind in (0, 1, 2):
        for c in range(CHUNKS):
            o_copy(others[kind], others[kind], c).wait_recv()
            for h in range(c * chunk, (c + 1) * chunk):
                merged[h] = merged[h] + shares[kind + 1][:, h : h + 1] * out_recv[
                    others[kind], c, :, head(h - c * chunk)
                ].astype(F32)
    for h in range(heads):
        both_ref[1, :, head(h)] = merged[h].astype(BF16)

    for other in others:
        for c in range(CHUNKS):
            o_copy(other, me, c).wait_send()
        s_copy(other, me).wait_send()

    def q_ends(device):
        for slot in range(len(sent_q[device])):
            for c in range(CHUNKS):
                q_copy(slot, *sent_q[device][slot], c).wait_send()

    for device in range(n):
        on(device, functools.partial(q_ends, device))
    on(0, lambda: (f_copy(0).wait_send(), f_copy(1).wait_send(), None)[-1])
    on(1, lambda: f_copy(2).wait_send())
    on(2, lambda: carry_copy().wait_send())


def four_shards(
    streams,
    history,
    filters,
    skip_weight,
    offset,
    lengths,
    queries,
    block_kv,
    cache_keys,
    cache_values,
):
    n = 4
    rows, channels = queries.shape
    groups, taps = filters.shape
    cache_rows = cache_keys.shape[0]
    span = cache_rows + LANES
    wide = channels // CHUNKS
    any_space = pl.BlockSpec(memory_space=pl.ANY)
    smem = pl.BlockSpec(memory_space=pltpu.SMEM)
    vmem = pl.BlockSpec(memory_space=pltpu.VMEM)
    dma = pltpu.SemaphoreType.DMA
    in_hbm = [
        pltpu.with_memory_space_constraint(x, pltpu.HBM)
        for x in (
            streams,
            history,
            filters,
            skip_weight,
            queries,
            block_kv,
            cache_keys,
            cache_values,
        )
    ]
    both = pl.pallas_call(
        kernel_of_four,
        out_shape=jax.ShapeDtypeStruct((2, rows, channels), BF16),
        in_specs=[smem, smem] + [any_space] * 8,
        out_specs=vmem,
        scratch_shapes=[
            pltpu.VMEM(streams.shape, BF16),
            pltpu.VMEM(history.shape, BF16),
            pltpu.VMEM(filters.shape, BF16),
            pltpu.VMEM((channels,), BF16),
            pltpu.VMEM((rows, channels), BF16),
            pltpu.VMEM(block_kv.shape, BF16),
            pltpu.VMEM((span, channels), BF16),
            pltpu.VMEM((span, channels), BF16),
            pltpu.VMEM((channels, span), BF16),
            pltpu.VMEM((taps, channels), F32),
            pltpu.VMEM((taps + n * rows, channels), BF16),
            pltpu.VMEM((groups * rows, 2 * taps), BF16),
            pltpu.VMEM((n, CHUNKS, rows, wide), BF16),
            pltpu.VMEM((n, CHUNKS, rows, wide), BF16),
            pltpu.VMEM((n, CHUNKS, rows, wide), BF16),
            pltpu.VMEM((n, 8, LANES), F32),
            pltpu.VMEM((n, 8, LANES), F32),
            pltpu.VMEM((rows, channels), BF16),
            pltpu.VMEM((rows, channels), BF16),
            dma((8,)),
            dma((5, CHUNKS)),
            dma((n, CHUNKS)),
            dma((4,)),
            dma((4,)),
            dma((n, CHUNKS)),
            dma((n, CHUNKS)),
            dma((n,)),
            dma((n,)),
            pltpu.SemaphoreType.REGULAR,
        ],
        compiler_params=pltpu.CompilerParams(
            collective_id=0, has_side_effects=True, vmem_limit_bytes=VMEM_LIMIT
        ),
    )(
        offset,
        lengths,
        *in_hbm,
    )
    return both[0], both[1]


def shards(
    n,
    streams,
    history,
    filters,
    skip_weight,
    offset,
    lengths,
    queries,
    block_kv,
    cache_keys,
    cache_values,
):
    rows, channels = queries.shape
    groups, taps = filters.shape
    cache_rows = cache_keys.shape[0]
    span = cache_rows + LANES
    if n == 4:
        return four_shards(
            streams,
            history,
            filters,
            skip_weight,
            offset,
            lengths,
            queries,
            block_kv,
            cache_keys,
            cache_values,
        )
    any_space = pl.BlockSpec(memory_space=pl.ANY)
    smem = pl.BlockSpec(memory_space=pltpu.SMEM)
    vmem = pl.BlockSpec(memory_space=pltpu.VMEM)
    dma = pltpu.SemaphoreType.DMA
    in_hbm = [
        pltpu.with_memory_space_constraint(x, pltpu.HBM)
        for x in (
            streams,
            history,
            filters,
            skip_weight,
            queries,
            block_kv,
            cache_keys,
            cache_values,
        )
    ]
    both = pl.pallas_call(
        functools.partial(kernel, n),
        out_shape=jax.ShapeDtypeStruct((2, rows, channels), BF16),
        in_specs=[smem, smem] + [any_space] * 8,
        out_specs=vmem,
        scratch_shapes=[
            pltpu.VMEM(streams.shape, BF16),
            pltpu.VMEM(history.shape, BF16),
            pltpu.VMEM(filters.shape, BF16),
            pltpu.VMEM((channels,), BF16),
            pltpu.VMEM((rows, channels), BF16),
            pltpu.VMEM(block_kv.shape, BF16),
            pltpu.VMEM((span, channels), BF16),
            pltpu.VMEM((span, channels), BF16),
            pltpu.VMEM((taps, channels), F32),
            pltpu.VMEM((taps + n * rows, channels), BF16),
            pltpu.VMEM((groups * rows, 2 * taps), BF16),
            pltpu.VMEM((n, rows, channels), BF16),
            pltpu.VMEM((n, rows, channels), BF16),
            pltpu.VMEM((n, rows, channels), BF16),
            pltpu.VMEM((n, 8, LANES), F32),
            pltpu.VMEM((n, 8, LANES), F32),
            dma((8,)),
            dma((n,)),
            dma((n,)),
            dma((n,)),
            dma((n,)),
            dma((n,)),
            dma((n,)),
            dma((n,)),
            dma((n,)),
        ],
        compiler_params=pltpu.CompilerParams(
            collective_id=0, has_side_effects=True, vmem_limit_bytes=VMEM_LIMIT
        ),
    )(
        offset,
        lengths,
        *in_hbm,
    )
    return both[0], both[1]


def solution(mesh):
    return jax.shard_map(
        functools.partial(shards, mesh.shape["ctx"]),
        mesh=mesh,
        in_specs=(
            P(None, ("seqs", "ctx"), ("head", "sub")),
            P("seqs", ("head", "sub")),
            P(("head", "sub"), None),
            P(("head", "sub")),
            P("seqs"),
            P(("seqs", "ctx")),
            P(("seqs", "ctx"), ("head", "sub")),
            P(None, ("seqs", "ctx"), ("head", "sub")),
            P(("seqs", "ctx"), ("head", "sub")),
            P(("seqs", "ctx"), ("head", "sub")),
        ),
        out_specs=(P(("seqs", "ctx"), ("head", "sub")), P(("seqs", "ctx"), ("head", "sub"))),
        check_vma=False,
    )
```

```python
import functools
import math

import jax
import jax.numpy as jnp
from jax import lax
from jax.experimental import pallas as pl
from jax.experimental.pallas import tpu as pltpu
from jax.sharding import PartitionSpec as P

HDIM = 128
ROPE_BASE = 1000000.0
MASKED = -1e30
MESH = pl.DeviceIdType.MESH
F32 = jnp.float32
BF16 = jnp.bfloat16
LANES = 128
CHUNKS = 2
VMEM_LIMIT = 32 * 2**20
EXPONENT = math.log2(math.e) / math.sqrt(HDIM)


def cos_sin(x):
    quarter = jnp.floor(x * (2.0 / math.pi) + 0.5)
    r = x - quarter * 1.5703125
    r = r - quarter * 4.837512969970703125e-4
    r = r - quarter * 7.54978995489188216e-8
    z = r * r
    sine = ((-1.9515295891e-4 * z + 8.3321608736e-3) * z - 1.6666654611e-1) * z * r + r
    cosine = (
        ((2.443315711809948e-5 * z - 1.388731625493765e-3) * z + 4.166664568298827e-2) * z * z
        - 0.5 * z
        + 1.0
    )
    turn = quarter.astype(jnp.int32) & 3
    odd = (turn & 1) == 1
    cos_x = jnp.where(odd, sine, cosine)
    sin_x = jnp.where(odd, cosine, sine)
    cos_x = jnp.where((turn == 1) | (turn == 2), -cos_x, cos_x)
    sin_x = jnp.where(turn >= 2, -sin_x, sin_x)
    return cos_x, sin_x


def kernel(
    n,
    offset_ref,
    lengths_ref,
    streams_hbm,
    history_hbm,
    filters_hbm,
    skip_hbm,
    queries_hbm,
    kv_hbm,
    keys_hbm,
    values_hbm,
    both_ref,
    streams,
    history,
    filters,
    skip,
    queries,
    kv,
    keys,
    values,
    history_wide,
    extended,
    toeplitz,
    all_q,
    out_send,
    out_recv,
    stat_send,
    stat_recv,
    in_sems,
    q_send,
    q_recv,
    f_send,
    f_recv,
    o_send,
    o_recv,
    s_send,
    s_recv,
):
    me = lax.axis_index("ctx")
    rows, channels = queries.shape
    heads = channels // HDIM
    groups, taps = filters.shape
    cache_rows = keys_hbm.shape[0]
    span = keys.shape[0]
    tile_groups = LANES // (channels // groups)

    barrier = pltpu.get_barrier_semaphore()
    for i in range(1, n):
        pl.semaphore_signal(
            barrier, inc=1, device_id={"ctx": lax.rem(me + i, n)}, device_id_type=MESH
        )

    loads = [
        pltpu.make_async_copy(source, target, in_sems.at[i])
        for i, (source, target) in enumerate(
            [
                (queries_hbm, queries),
                (streams_hbm, streams),
                (kv_hbm, kv),
                (filters_hbm, filters),
                (history_hbm, history),
                (skip_hbm, skip),
                (keys_hbm, keys.at[pl.ds(0, cache_rows)]),
                (values_hbm, values.at[pl.ds(0, cache_rows)]),
            ]
        )
    ]
    for load in loads:
        load.start()

    position = (
        offset_ref[0] + me * rows + lax.broadcasted_iota(jnp.int32, (rows, HDIM), 0)
    ).astype(F32)
    lane = lax.broadcasted_iota(jnp.int32, (rows, HDIM), 1)
    pair = lax.broadcasted_iota(jnp.int32, (8, HDIM), 1) % (HDIM // 2)
    freq = jnp.ones((8, HDIM), F32)
    for i in range(1, HDIM // 2):
        freq = jnp.where(pair == i, float(1.0 / ROPE_BASE ** (2.0 * i / HDIM)), freq)
    cosine, sine = cos_sin(position * freq[0:1, :])
    sine = jnp.where(lane < HDIM // 2, -sine, sine)

    def rotated(x):
        x = x.astype(F32)
        return (x * cosine + pltpu.roll(x, HDIM // 2, 1) * sine).astype(BF16)

    loads[0].wait()
    for h in range(heads):
        part = slice(h * HDIM, (h + 1) * HDIM)
        all_q[me, :, part] = rotated(queries[:, part])

    pl.semaphore_wait(barrier, n - 1)

    def flipped(i):
        result = me
        for b in [1 << k for k in range(n.bit_length()) if i >> k & 1]:
            result = result + b * (1 - 2 * lax.rem(lax.div(me, b), 2))
        return result

    def children(i):
        low = i & -i if i else n
        return [i + (1 << k) for k in reversed(range(n.bit_length())) if (1 << k) < low]

    def q_copy(i):
        low = i & -i
        block = flipped(i - low)
        return pltpu.make_async_remote_copy(
            src_ref=all_q.at[block],
            dst_ref=all_q.at[block],
            send_sem=q_send.at[i],
            recv_sem=q_recv.at[i],
            device_id={"ctx": flipped(low)},
            device_id_type=MESH,
        )

    for i in children(0):
        q_copy(i).start()

    loads[1].wait()
    own_rows = pl.ds(pl.multiple_of(taps + me * rows, rows), rows)
    extended[own_rows, :] = (streams[1].astype(F32) * streams[2].astype(F32)).astype(BF16)

    def f_copy(i):
        low = i & -i
        start = pl.multiple_of(taps + flipped(i - low) * rows, rows)
        return pltpu.make_async_remote_copy(
            src_ref=extended.at[pl.ds(start, rows)],
            dst_ref=extended.at[pl.ds(start, rows)],
            send_sem=f_send.at[i],
            recv_sem=f_recv.at[i],
            device_id={"ctx": flipped(low)},
            device_id_type=MESH,
        )

    def f_start(i):
        low = i & -i

        @pl.when(flipped(i - low) < flipped(low))
        def _():
            f_copy(i).start()

    def f_take(i):
        @pl.when(flipped(i) < me)
        def _():
            f_copy(i).wait_recv()

        for j in children(i):
            f_start(j)

    def q_take(i):
        q_copy(i).wait_recv()
        for j in children(i):
            q_copy(j).start()

    for i in children(0):
        f_start(i)

    loads[2].wait()
    for h in range(heads):
        part = slice(h * HDIM, (h + 1) * HDIM)
        keys[pl.ds(cache_rows, rows), part] = rotated(kv[0, :, part])
    values[pl.ds(cache_rows, rows), :] = kv[1]
    pad = span - cache_rows - rows
    keys[pl.ds(cache_rows + rows, pad), :] = jnp.zeros((pad, channels), BF16)
    values[pl.ds(cache_rows + rows, pad), :] = jnp.zeros((pad, channels), BF16)

    loads[3].wait()
    mirror = (
        lax.broadcasted_iota(jnp.int32, (taps, 2 * taps), 1)
        + lax.broadcasted_iota(jnp.int32, (taps, 2 * taps), 0)
        == taps
    ).astype(BF16)
    base = jnp.dot(filters[...], mirror, preferred_element_type=F32)
    for g in range(groups):
        line = jnp.broadcast_to(base[g : g + 1, :], (rows, 2 * taps))
        toeplitz[g * rows : (g + 1) * rows, :] = pltpu.roll(
            line, 0, 1, stride=1, stride_axis=0
        ).astype(BF16)

    loads[4].wait()
    history_wide[0:1, :] = jnp.zeros((1, channels), F32)
    history_wide[1:taps, :] = history[...].astype(F32)
    extended[0:taps, :] = history_wide[...].astype(BF16)
    loads[5].wait()

    loads[6].wait()
    loads[7].wait()
    column = lax.broadcasted_iota(jnp.int32, (rows, span), 1)
    token = lax.broadcasted_iota(jnp.int32, (rows, span), 0)
    length = lengths_ref[0]

    def attend(source):
        kept = (column < jnp.minimum(length, cache_rows)) | (
            (column >= cache_rows)
            & (column < cache_rows + rows)
            & (column - cache_rows + me * rows <= token + source * rows)
        )
        bias = jnp.where(kept, 0.0, MASKED)
        stat = jnp.zeros((rows, LANES), F32)
        parts = [slice(h * HDIM, (h + 1) * HDIM) for h in range(heads)]
        scores = [
            lax.dot_general(
                all_q[source, :, part],
                keys[:, part],
                (((1,), (1,)), ((), ())),
                preferred_element_type=F32,
            )
            + bias
            for part in parts
        ]
        tops = [jnp.max(score, axis=1, keepdims=True) for score in scores]
        weights = [
            jnp.exp2((score - top) * EXPONENT) for score, top in zip(scores, tops)
        ]
        totals = [jnp.sum(weight, axis=1, keepdims=True) for weight in weights]
        sums = [
            jnp.dot(weight.astype(BF16), values[:, part], preferred_element_type=F32)
            for weight, part in zip(weights, parts)
        ]
        for h in range(heads):
            out_send[source, :, parts[h]] = (sums[h] / totals[h]).astype(BF16)
            stat = jnp.where(lane == h, tops[h], stat)
            stat = jnp.where(lane == heads + h, totals[h], stat)
        packed = stat[0:8]
        for a in range(1, rows // 8):
            packed = packed + pltpu.roll(stat[8 * a : 8 * a + 8], 2 * heads * a, 1)
        stat_send[source] = packed

    def o_copy(i, source):
        return pltpu.make_async_remote_copy(
            src_ref=out_send.at[source],
            dst_ref=out_recv.at[me],
            send_sem=o_send.at[i],
            recv_sem=o_recv.at[i],
            device_id={"ctx": source},
            device_id_type=MESH,
        )

    def s_copy(i, source):
        return pltpu.make_async_remote_copy(
            src_ref=stat_send.at[source],
            dst_ref=stat_recv.at[me],
            send_sem=s_send.at[i],
            recv_sem=s_recv.at[i],
            device_id={"ctx": source},
            device_id_type=MESH,
        )

    def attend_and_send(i, source):
        attend(source)
        s_copy(i, source).start()
        o_copy(i, source).start()

    attend(me)
    if n == 4:
        q_take(2)
        q_take(1)
        attend_and_send(1, flipped(1))
        f_take(2)
        attend_and_send(2, flipped(2))
        q_take(3)
        attend_and_send(3, flipped(3))
        f_take(1)
        f_take(3)
    else:
        for i in sorted(range(1, n), key=lambda i: i.bit_count()):
            q_take(i)
            f_take(i)

        def step(i, _):
            attend_and_send(i, lax.rem(me - i + n, n))
            return 0

        lax.fori_loop(1, n, step, 0)

    direct = skip[...].astype(F32).reshape(1, channels)
    lane_group = lane // (channels // groups)
    for j in range(channels // LANES):
        part = slice(j * LANES, (j + 1) * LANES)
        stack = slice(j * tile_groups * rows, (j + 1) * tile_groups * rows)
        own = extended[own_rows, part]
        window = extended[pl.ds(pl.multiple_of(me * rows, rows), taps), part]
        product = jnp.dot(
            toeplitz[stack, 0:taps], window, preferred_element_type=F32
        ) + jnp.dot(toeplitz[stack, taps : taps + rows], own, preferred_element_type=F32)
        conv = product[0:rows]
        for g in range(1, tile_groups):
            conv = jnp.where(lane_group == g, product[g * rows : (g + 1) * rows], conv)
        both_ref[0, :, part] = (
            streams[0, :, part].astype(F32)
            * (conv + direct[:, part] * own.astype(F32))
        ).astype(BF16)

    for i in range(1, n):
        s_copy(i, me).wait_recv()

    stat_recv[me] = stat_send[me]
    def source_of(i):
        return flipped(i) if n == 4 else lax.rem(me + i, n)

    stats = []
    for i in range(n):
        packed = stat_recv[source_of(i)]
        stats.append(
            jnp.concatenate(
                [packed]
                + [
                    pltpu.roll(packed, LANES - 2 * heads * a, 1)
                    for a in range(1, rows // 8)
                ],
                axis=0,
            )
        )
    top = stats[0]
    for s in range(1, n):
        top = jnp.maximum(top, stats[s])
    shares = []
    whole = jnp.zeros((rows, LANES), F32)
    for s in range(n):
        stat = stats[s]
        count = pltpu.roll(stat, LANES - heads, 1)
        share = jnp.exp2((stat - top) * EXPONENT) * count
        share = jnp.where(lane < heads, share, 0.0)
        shares.append(share)
        whole = whole + share
    inverse = 1.0 / jnp.where(lane < heads, whole, 1.0)
    shares = [share * inverse for share in shares]
    merged = [jnp.zeros((rows, HDIM), F32)] * heads
    for i in range(n):
        if i:
            o_copy(i, me).wait_recv()
        came = out_recv.at[source_of(i)] if i else out_send.at[me]
        for h in range(heads):
            part = slice(h * HDIM, (h + 1) * HDIM)
            merged[h] = merged[h] + shares[i][:, h : h + 1] * came[:, part].astype(F32)
    for h in range(heads):
        both_ref[1, :, h * HDIM : (h + 1) * HDIM] = merged[h].astype(BF16)

    for i in range(1, n):
        q_copy(i).wait_send()
        o_copy(i, me).wait_send()
        s_copy(i, me).wait_send()
        low = i & -i

        @pl.when(flipped(i - low) < flipped(low))
        def _(i=i):
            f_copy(i).wait_send()


def kernel_of_four(
    offset_ref,
    lengths_ref,
    streams_hbm,
    history_hbm,
    filters_hbm,
    skip_hbm,
    queries_hbm,
    kv_hbm,
    keys_hbm,
    values_hbm,
    both_ref,
    streams,
    history,
    filters,
    skip,
    queries,
    kv,
    keys,
    values,
    keys_across,
    history_wide,
    extended,
    toeplitz,
    all_q,
    out_send,
    out_recv,
    stat_send,
    stat_recv,
    carry_send,
    carry,
    in_sems,
    q_send,
    q_recv,
    f_send,
    f_recv,
    o_send,
    o_recv,
    s_send,
    s_recv,
    join,
):
    n = 4
    me = lax.axis_index("ctx")
    rows, channels = queries.shape
    heads = channels // HDIM
    groups, taps = filters.shape
    cache_rows = keys_hbm.shape[0]
    span = keys.shape[0]
    tile_groups = LANES // (channels // groups)
    chunk = heads // CHUNKS

    last = n - 1
    first = jnp.where(me == 0, 1, jnp.where(me == 1, 0, jnp.where(me == 2, 1, 2)))
    second = jnp.where(me < 2, 2, 0)
    third = jnp.where(me == last, 1, last)
    others = [first, second, third]

    barrier = pltpu.get_barrier_semaphore()

    @pl.when(me != last)
    def _():
        for i in range(1, n):
            pl.semaphore_signal(
                barrier,
                inc=1,
                device_id={"ctx": lax.rem(me + i, n)},
                device_id_type=MESH,
            )

    loads = [
        pltpu.make_async_copy(source, target, in_sems.at[i])
        for i, (source, target) in enumerate(
            [
                (queries_hbm, queries),
                (streams_hbm, streams),
                (kv_hbm, kv),
                (filters_hbm, filters),
                (history_hbm, history),
                (skip_hbm, skip),
                (keys_hbm, keys.at[pl.ds(0, cache_rows)]),
                (values_hbm, values.at[pl.ds(0, cache_rows)]),
            ]
        )
    ]
    for load in loads:
        load.start()

    position = (
        offset_ref[0] + me * rows + lax.broadcasted_iota(jnp.int32, (rows, HDIM), 0)
    ).astype(F32)
    lane = lax.broadcasted_iota(jnp.int32, (rows, HDIM), 1)
    pair = lax.broadcasted_iota(jnp.int32, (8, HDIM), 1) % (HDIM // 2)
    freq = jnp.ones((8, HDIM), F32)
    for i in range(1, HDIM // 2):
        freq = jnp.where(pair == i, float(1.0 / ROPE_BASE ** (2.0 * i / HDIM)), freq)
    cosine, sine = cos_sin(position * freq[0:1, :])
    sine = jnp.where(lane < HDIM // 2, -sine, sine)

    def rotated(x):
        x = x.astype(F32)
        return (x * cosine + pltpu.roll(x, HDIM // 2, 1) * sine).astype(BF16)

    def head(h):
        return slice(h * HDIM, (h + 1) * HDIM)

    loads[0].wait()
    for h in range(heads):
        all_q[me, h // chunk, :, head(h % chunk)] = rotated(queries[:, head(h)])

    def on(device, action):
        pl.when(me == device)(action)

    pl.semaphore_wait(barrier, jnp.where(me == last, n - 1, n - 2))

    @pl.when(me == last)
    def _():
        for i in range(n - 1):
            pl.semaphore_signal(
                join, inc=1, device_id={"ctx": i}, device_id_type=MESH
            )

    def q_copy(slot, block, target, c):
        return pltpu.make_async_remote_copy(
            src_ref=all_q.at[block, c],
            dst_ref=all_q.at[block, c],
            send_sem=q_send.at[slot, c],
            recv_sem=q_recv.at[block, c],
            device_id={"ctx": target},
            device_id_type=MESH,
        )

    def q_take(block, c):
        q_copy(0, block, lax.rem(me + 1, n), c).wait_recv()

    sent_q = [
        [(0, 2), (0, 1), (0, 3)],
        [(1, 2), (1, 0)],
        [(2, 0), (2, 1), (2, 3), (1, 3)],
        [(3, 0), (3, 1), (3, 2)],
    ]

    def q_starts(device, slots):
        for slot in slots:
            for c in range(CHUNKS):
                q_copy(slot, *sent_q[device][slot], c).start()

    for device in range(n):
        on(device, functools.partial(q_starts, device, (0, 1, 2) if device == 3 else (0, 1)))

    loads[1].wait()
    own_rows = pl.ds(pl.multiple_of(taps + me * rows, rows), rows)
    extended[own_rows, :] = (streams[1].astype(F32) * streams[2].astype(F32)).astype(BF16)

    passed = [(0, 1), (0, 2), (1, 2)]

    def f_copy(i):
        source, target = passed[i]
        block = extended.at[pl.ds(taps + source * rows, rows)]
        return pltpu.make_async_remote_copy(
            src_ref=block,
            dst_ref=block,
            send_sem=f_send.at[i],
            recv_sem=f_recv.at[i],
            device_id={"ctx": target},
            device_id_type=MESH,
        )

    def carry_copy():
        return pltpu.make_async_remote_copy(
            src_ref=carry_send,
            dst_ref=carry,
            send_sem=f_send.at[3],
            recv_sem=f_recv.at[3],
            device_id={"ctx": 3},
            device_id_type=MESH,
        )

    def f_starts():
        on(0, lambda: (f_copy(1).start(), f_copy(0).start(), None)[-1])
        on(1, lambda: f_copy(2).start())


    @pl.when(me == 3)
    def _():
        extended[taps : taps + 3 * rows, :] = jnp.zeros((3 * rows, channels), BF16)

    @pl.when(me != 3)
    def _():
        carry[...] = jnp.zeros((rows, channels), BF16)

    loads[2].wait()
    for h in range(heads):
        keys[pl.ds(cache_rows, rows), head(h)] = rotated(kv[0, :, head(h)])
    values[pl.ds(cache_rows, rows), :] = kv[1]
    pad = span - cache_rows - rows
    keys[pl.ds(cache_rows + rows, pad), :] = jnp.zeros((pad, channels), BF16)
    values[pl.ds(cache_rows + rows, pad), :] = jnp.zeros((pad, channels), BF16)

    @pl.when(me == 2)
    def _():
        pl.semaphore_wait(join, 1)
        q_starts(2, (2,))

    loads[3].wait()
    mirror = (
        lax.broadcasted_iota(jnp.int32, (taps, 2 * taps), 1)
        + lax.broadcasted_iota(jnp.int32, (taps, 2 * taps), 0)
        == taps
    ).astype(BF16)
    base = jnp.dot(filters[...], mirror, preferred_element_type=F32)
    for g in range(groups):
        line = jnp.broadcast_to(base[g : g + 1, :], (rows, 2 * taps))
        toeplitz[g * rows : (g + 1) * rows, :] = pltpu.roll(
            line, 0, 1, stride=1, stride_axis=0
        ).astype(BF16)

    loads[4].wait()
    history_wide[0:1, :] = jnp.zeros((1, channels), F32)
    history_wide[1:taps, :] = history[...].astype(F32)
    extended[0:taps, :] = history_wide[...].astype(BF16)
    loads[5].wait()

    loads[6].wait()
    for h in range(heads):
        keys_across[head(h), :] = keys[:, head(h)].T
    loads[7].wait()
    length = lengths_ref[0]
    cached = lax.broadcasted_iota(jnp.int32, (8, cache_rows), 1)
    cache_bias = jnp.where(cached < length, 0.0, MASKED)[0:1, :]
    block_column = lax.broadcasted_iota(jnp.int32, (rows, span - cache_rows), 1)
    block_token = lax.broadcasted_iota(jnp.int32, (rows, span - cache_rows), 0)

    def attend(source, mine, stat):
        kept = (block_column < rows) & (
            block_column + me * rows <= block_token + source * rows
        )
        block_bias = jnp.where(kept, 0.0, MASKED)
        scores = [
            jnp.dot(
                all_q[source, h // chunk, :, head(h % chunk)],
                keys_across[head(h), :],
                preferred_element_type=F32,
            )
            for h in mine
        ]
        scores = [
            jnp.concatenate(
                [score[:, :cache_rows] + cache_bias, score[:, cache_rows:] + block_bias],
                axis=1,
            )
            for score in scores
        ]
        tops = [jnp.max(score, axis=1, keepdims=True) for score in scores]
        weights = [
            jnp.exp2((score - top) * EXPONENT) for score, top in zip(scores, tops)
        ]
        totals = [jnp.sum(weight, axis=1, keepdims=True) for weight in weights]
        sums = [
            jnp.dot(weight.astype(BF16), values[:, head(h)], preferred_element_type=F32)
            for weight, h in zip(weights, mine)
        ]
        for i, h in enumerate(mine):
            out_send[source, h // chunk, :, head(h % chunk)] = (
                sums[i] / totals[i]
            ).astype(BF16)
            stat = jnp.where(lane == h, tops[i], stat)
            stat = jnp.where(lane == heads + h, totals[i], stat)
        return stat

    def packed(stat):
        result = stat[0:8]
        for a in range(1, rows // 8):
            result = result + pltpu.roll(stat[8 * a : 8 * a + 8], 2 * heads * a, 1)
        return result

    def o_copy(other, source, c):
        return pltpu.make_async_remote_copy(
            src_ref=out_send.at[other, c],
            dst_ref=out_recv.at[me, c],
            send_sem=o_send.at[other, c],
            recv_sem=o_recv.at[source, c],
            device_id={"ctx": other},
            device_id_type=MESH,
        )

    def s_copy(other, source):
        return pltpu.make_async_remote_copy(
            src_ref=stat_send.at[other],
            dst_ref=stat_recv.at[me],
            send_sem=s_send.at[other],
            recv_sem=s_recv.at[source],
            device_id={"ctx": other},
            device_id_type=MESH,
        )

    def conv_tile(j, window):
        stack = slice(j * tile_groups * rows, (j + 1) * tile_groups * rows)
        return jnp.dot(toeplitz[stack, 0:taps], window, preferred_element_type=F32)

    lane_group = lane // (channels // groups)

    def picked(product):
        conv = product[0:rows]
        for g in range(1, tile_groups):
            conv = jnp.where(lane_group == g, product[g * rows : (g + 1) * rows], conv)
        return conv

    def take_filter_inputs():
        on(1, lambda: f_copy(0).wait_recv())

        @pl.when(me == 2)
        def _():
            f_copy(1).wait_recv()
            f_copy(2).wait_recv()
            for j in range(channels // LANES):
                part = slice(j * LANES, (j + 1) * LANES)
                window = jnp.concatenate(
                    [
                        jnp.zeros((taps - 3 * rows, LANES), BF16),
                        extended[taps : taps + 3 * rows, part],
                    ],
                    axis=0,
                )
                carry_send[:, part] = picked(conv_tile(j, window)).astype(BF16)
            carry_copy().start()

    nothing = jnp.zeros((rows, LANES), F32)
    def attend_and_send(other):
        stat_send[other] = packed(attend(other, range(heads), nothing))
        s_copy(other, me).start()
        for c in range(CHUNKS):
            o_copy(other, me, c).start()

    def take_all(block):
        for c in range(CHUNKS):
            q_take(block, c)

    def pass_on(device, slot):
        block = sent_q[device][slot][0]
        for c in range(CHUNKS):
            q_take(block, c)
            q_copy(slot, *sent_q[device][slot], c).start()

    @pl.when(me == 0)
    def _():
        pl.semaphore_wait(join, 1)
        q_starts(0, (2,))

    stat_send[me] = packed(attend(me, range(heads), nothing))

    on(2, lambda: pass_on(2, 3))

    @pl.when(me != 2)
    def _():
        take_all(first)

    f_starts()
    attend_and_send(first)
    take_all(second)
    attend_and_send(second)
    take_filter_inputs()
    on(1, lambda: pl.semaphore_wait(join, 1))
    take_all(third)
    attend_and_send(third)

    on(3, lambda: carry_copy().wait_recv())
    direct = skip[...].astype(F32).reshape(1, channels)
    for j in range(channels // LANES):
        part = slice(j * LANES, (j + 1) * LANES)
        stack = slice(j * tile_groups * rows, (j + 1) * tile_groups * rows)
        mine = extended[own_rows, part]
        window = extended[pl.ds(pl.multiple_of(me * rows, rows), taps), part]
        product = conv_tile(j, window) + jnp.dot(
            toeplitz[stack, taps : taps + rows], mine, preferred_element_type=F32
        )
        conv = picked(product) + carry[:, part].astype(F32)
        both_ref[0, :, part] = (
            streams[0, :, part].astype(F32)
            * (conv + direct[:, part] * mine.astype(F32))
        ).astype(BF16)

    for other in others:
        s_copy(other, other).wait_recv()

    def unpacked(value):
        return jnp.concatenate(
            [value]
            + [
                pltpu.roll(value, LANES - 2 * heads * a, 1) for a in range(1, rows // 8)
            ],
            axis=0,
        )

    came = [unpacked(stat_send[me])] + [unpacked(stat_recv[other]) for other in others]
    top = came[0]
    for stat in came[1:]:
        top = jnp.maximum(top, stat)
    shares = []
    whole = jnp.zeros((rows, LANES), F32)
    for stat in came:
        count = pltpu.roll(stat, LANES - heads, 1)
        share = jnp.exp2((stat - top) * EXPONENT) * count
        share = jnp.where(lane < heads, share, 0.0)
        shares.append(share)
        whole = whole + share
    inverse = 1.0 / jnp.where(lane < heads, whole, 1.0)
    shares = [share * inverse for share in shares]
    merged = [
        shares[0][:, h : h + 1]
        * out_send[me, h // chunk, :, head(h % chunk)].astype(F32)
        for h in range(heads)
    ]
    for kind in (0, 1, 2):
        for c in range(CHUNKS):
            o_copy(others[kind], others[kind], c).wait_recv()
            for h in range(c * chunk, (c + 1) * chunk):
                merged[h] = merged[h] + shares[kind + 1][:, h : h + 1] * out_recv[
                    others[kind], c, :, head(h - c * chunk)
                ].astype(F32)
    for h in range(heads):
        both_ref[1, :, head(h)] = merged[h].astype(BF16)

    for other in others:
        for c in range(CHUNKS):
            o_copy(other, me, c).wait_send()
        s_copy(other, me).wait_send()

    def q_ends(device):
        for slot in range(len(sent_q[device])):
            for c in range(CHUNKS):
                q_copy(slot, *sent_q[device][slot], c).wait_send()

    for device in range(n):
        on(device, functools.partial(q_ends, device))
    on(0, lambda: (f_copy(0).wait_send(), f_copy(1).wait_send(), None)[-1])
    on(1, lambda: f_copy(2).wait_send())
    on(2, lambda: carry_copy().wait_send())


def four_shards(
    streams,
    history,
    filters,
    skip_weight,
    offset,
    lengths,
    queries,
    block_kv,
    cache_keys,
    cache_values,
):
    n = 4
    rows, channels = queries.shape
    groups, taps = filters.shape
    cache_rows = cache_keys.shape[0]
    span = cache_rows + LANES
    wide = channels // CHUNKS
    any_space = pl.BlockSpec(memory_space=pl.ANY)
    smem = pl.BlockSpec(memory_space=pltpu.SMEM)
    vmem = pl.BlockSpec(memory_space=pltpu.VMEM)
    dma = pltpu.SemaphoreType.DMA
    in_hbm = [
        pltpu.with_memory_space_constraint(x, pltpu.HBM)
        for x in (
            streams,
            history,
            filters,
            skip_weight,
            queries,
            block_kv,
            cache_keys,
            cache_values,
        )
    ]
    both = pl.pallas_call(
        kernel_of_four,
        out_shape=jax.ShapeDtypeStruct((2, rows, channels), BF16),
        in_specs=[smem, smem] + [any_space] * 8,
        out_specs=vmem,
        scratch_shapes=[
            pltpu.VMEM(streams.shape, BF16),
            pltpu.VMEM(history.shape, BF16),
            pltpu.VMEM(filters.shape, BF16),
            pltpu.VMEM((channels,), BF16),
            pltpu.VMEM((rows, channels), BF16),
            pltpu.VMEM(block_kv.shape, BF16),
            pltpu.VMEM((span, channels), BF16),
            pltpu.VMEM((span, channels), BF16),
            pltpu.VMEM((channels, span), BF16),
            pltpu.VMEM((taps, channels), F32),
            pltpu.VMEM((taps + n * rows, channels), BF16),
            pltpu.VMEM((groups * rows, 2 * taps), BF16),
            pltpu.VMEM((n, CHUNKS, rows, wide), BF16),
            pltpu.VMEM((n, CHUNKS, rows, wide), BF16),
            pltpu.VMEM((n, CHUNKS, rows, wide), BF16),
            pltpu.VMEM((n, 8, LANES), F32),
            pltpu.VMEM((n, 8, LANES), F32),
            pltpu.VMEM((rows, channels), BF16),
            pltpu.VMEM((rows, channels), BF16),
            dma((8,)),
            dma((5, CHUNKS)),
            dma((n, CHUNKS)),
            dma((4,)),
            dma((4,)),
            dma((n, CHUNKS)),
            dma((n, CHUNKS)),
            dma((n,)),
            dma((n,)),
            pltpu.SemaphoreType.REGULAR,
        ],
        compiler_params=pltpu.CompilerParams(
            collective_id=0, has_side_effects=True, vmem_limit_bytes=VMEM_LIMIT
        ),
    )(
        offset,
        lengths,
        *in_hbm,
    )
    return both[0], both[1]


def shards(
    n,
    streams,
    history,
    filters,
    skip_weight,
    offset,
    lengths,
    queries,
    block_kv,
    cache_keys,
    cache_values,
):
    rows, channels = queries.shape
    groups, taps = filters.shape
    cache_rows = cache_keys.shape[0]
    span = cache_rows + LANES
    if n == 4:
        return four_shards(
            streams,
            history,
            filters,
            skip_weight,
            offset,
            lengths,
            queries,
            block_kv,
            cache_keys,
            cache_values,
        )
    any_space = pl.BlockSpec(memory_space=pl.ANY)
    smem = pl.BlockSpec(memory_space=pltpu.SMEM)
    vmem = pl.BlockSpec(memory_space=pltpu.VMEM)
    dma = pltpu.SemaphoreType.DMA
    in_hbm = [
        pltpu.with_memory_space_constraint(x, pltpu.HBM)
        for x in (
            streams,
            history,
            filters,
            skip_weight,
            queries,
            block_kv,
            cache_keys,
            cache_values,
        )
    ]
    both = pl.pallas_call(
        functools.partial(kernel, n),
        out_shape=jax.ShapeDtypeStruct((2, rows, channels), BF16),
        in_specs=[smem, smem] + [any_space] * 8,
        out_specs=vmem,
        scratch_shapes=[
            pltpu.VMEM(streams.shape, BF16),
            pltpu.VMEM(history.shape, BF16),
            pltpu.VMEM(filters.shape, BF16),
            pltpu.VMEM((channels,), BF16),
            pltpu.VMEM((rows, channels), BF16),
            pltpu.VMEM(block_kv.shape, BF16),
            pltpu.VMEM((span, channels), BF16),
            pltpu.VMEM((span, channels), BF16),
            pltpu.VMEM((taps, channels), F32),
            pltpu.VMEM((taps + n * rows, channels), BF16),
            pltpu.VMEM((groups * rows, 2 * taps), BF16),
            pltpu.VMEM((n, rows, channels), BF16),
            pltpu.VMEM((n, rows, channels), BF16),
            pltpu.VMEM((n, rows, channels), BF16),
            pltpu.VMEM((n, 8, LANES), F32),
            pltpu.VMEM((n, 8, LANES), F32),
            dma((8,)),
            dma((n,)),
            dma((n,)),
            dma((n,)),
            dma((n,)),
            dma((n,)),
            dma((n,)),
            dma((n,)),
            dma((n,)),
        ],
        compiler_params=pltpu.CompilerParams(
            collective_id=0, has_side_effects=True, vmem_limit_bytes=VMEM_LIMIT
        ),
    )(
        offset,
        lengths,
        *in_hbm,
    )
    return both[0], both[1]


def solution(mesh):
    return jax.shard_map(
        functools.partial(shards, mesh.shape["ctx"]),
        mesh=mesh,
        in_specs=(
            P(None, ("seqs", "ctx"), ("head", "sub")),
            P("seqs", ("head", "sub")),
            P(("head", "sub"), None),
            P(("head", "sub")),
            P("seqs"),
            P(("seqs", "ctx")),
            P(("seqs", "ctx"), ("head", "sub")),
            P(None, ("seqs", "ctx"), ("head", "sub")),
            P(("seqs", "ctx"), ("head", "sub")),
            P(("seqs", "ctx"), ("head", "sub")),
        ),
        out_specs=(P(("seqs", "ctx"), ("head", "sub")), P(("seqs", "ctx"), ("head", "sub"))),
        check_vma=False,
    )
```
